32 devices in a mesh: seq: 8 (over z, y), head: 4 (over x, core).
Axes of the slice: x: 2, y: 2, z: 4, core: 2. Of those that a mesh axis runs over, the one named last changes fastest.
Arguments:
- query: bfloat16 [4096, 1024], P('seq', 'head'), may hold values from -70 to 70
- key: bfloat16 [4096, 1024], P('seq', 'head'), may hold values from -15 to 15
- value: bfloat16 [4096, 1024], P('seq', 'head'), may hold values from -6 to 6
- middle_offsets: int32 [16], P('head'), may hold values from 0 to 3
- upper_offsets: int32 [16], P('head'), may hold values from 0 to 3
- out_weight: bfloat16 [1024, 1024], P('head'), may hold values from -0.1875 to 0.1875
Outputs:
- projected: bfloat16 [4096, 1024], P(('seq', 'head'))
The draws below stay inside these ranges and needn't reach their ends.
All inputs are finite; a program needn't handle non-finite values.
Results may differ from the reference program's by a relative error of at most 0.0051.
Values may be sent and summed in bfloat16 or wider, within the bound.
A program may use at most 64 MiB of HBM per device.

```python
import jax
import jax.numpy as jnp
from jax import lax

D = 1024
HEAD_TOTAL = 16
HD = 64
TOKENS_PER_SHARD = 512
SPAN = 8
MIDDLE_DILATION = 4
TOP_DILATION = 4
TOKENS = 4096
N_SEQ = 8


def draw_query(key, part):
    normal_part = jnp.clip(jax.random.normal(jax.random.fold_in(key, 1), (TOKENS, HEAD_TOTAL * HD), jnp.float32), -6.0, 6.0)
    return normal_part.astype(jnp.bfloat16)


def draw_key(key, part):
    normal_part = jnp.clip(jax.random.normal(jax.random.fold_in(key, 3), (TOKENS, HEAD_TOTAL * HD), jnp.float32), -6.0, 6.0)
    return (normal_part * 2.5).astype(jnp.bfloat16)


def touch_ends(drawn, own_key, smallest, largest):
    longest = drawn.shape.index(max(drawn.shape))
    spots = []
    for shift in (0, 1):
        where = [jax.random.randint(jax.random.fold_in(own_key, axis), (), 0, length) for axis, length in enumerate(drawn.shape)]
        where[longest] = (where[longest] + shift) % drawn.shape[longest]
        spots.append(tuple(where))
    return drawn.at[spots[0]].set(smallest).at[spots[1]].set(largest)


def steps_of(own_key, extent, shards, low, largest):
    def one(position, blocks):
        draws = jax.random.uniform(jax.random.fold_in(jax.random.fold_in(own_key, 6), position), (blocks,), jnp.float32, low / len(shards), largest / len(shards))
        return jnp.repeat(jnp.exp(draws), extent[position] // blocks).reshape((-1,) + (1,) * (len(extent) - position - 1))

    loudness = one(*shards[0])
    for cut in shards[1:]:
        loudness = loudness * one(*cut)
    return loudness


def bell_draw(stream_key, extent, width, bound, cuts=(), held_as=jnp.bfloat16):
    values = jax.random.normal(stream_key, extent, jnp.float32) * width
    if len(cuts) > 0:
        values = steps_of(stream_key, extent, cuts, -0.22, 0.18) * values
    return jnp.clip(values, min=-bound, max=bound).astype(held_as)


def setup_inputs(seed: int = 0) -> dict:
    key_of = jax.random.split(jax.random.key(seed), 7)
    query = draw_query(jax.random.fold_in(key_of[6], 71), 0)
    key = draw_key(jax.random.fold_in(key_of[6], 71), 0)
    value = bell_draw(key_of[2], (TOKENS, HEAD_TOTAL * HD), 1.0, 6.0, ((0, 8), (1, 4)))
    middle_offsets = touch_ends(jax.random.randint(key_of[3], (HEAD_TOTAL,), 0, MIDDLE_DILATION), jax.random.fold_in(key_of[3], 1), 0, MIDDLE_DILATION - 1).astype(jnp.int32)
    upper_offsets = touch_ends(jax.random.randint(key_of[4], (HEAD_TOTAL,), 0, TOP_DILATION), jax.random.fold_in(key_of[4], 1), 0, TOP_DILATION - 1).astype(jnp.int32)
    out_weight = bell_draw(key_of[5], (HEAD_TOTAL * HD, D), (HEAD_TOTAL * HD) ** -0.5, 0.1875, ((0, 4),))
    return {"query": query, "key": key, "value": value, "middle_offsets": middle_offsets, "upper_offsets": upper_offsets, "out_weight": out_weight}


def attend_segment(query_matrix_rows, key_matrix_rows, value_matrix_rows):
    scores = jnp.einsum("qhd,khd->hqk", query_matrix_rows.astype(jnp.float32), key_matrix_rows.astype(jnp.float32)) * (HD ** -0.5)
    row_max = jnp.max(scores, axis=2)
    mass = jnp.exp(scores - row_max[:, :, None])
    total = jnp.sum(mass, axis=2)
    soft_weights = mass.astype(jnp.bfloat16)
    weighted = jnp.einsum("hqk,khd->qhd", soft_weights.astype(jnp.float32), value_matrix_rows.astype(jnp.float32))
    return weighted, total.T, row_max.T


def attend_trio(trio):
    return attend_segment(trio[0], trio[1], trio[2])


def picked_rows(block_rows, offsets, stride):
    group_count = block_rows.shape[0] // stride
    grouped = block_rows.reshape(group_count, stride, block_rows.shape[1], block_rows.shape[2])
    gather_index = jnp.broadcast_to(offsets.astype(jnp.int32)[None, None, :, None], (group_count, 1, block_rows.shape[1], block_rows.shape[2]))
    return jnp.take_along_axis(grouped, gather_index, axis=1)[:, 0]


def scatter_rows(values, offsets, stride, filler):
    chosen = jnp.arange(stride, dtype=jnp.int32)[:, None] == offsets.astype(jnp.int32)[None, :]
    chosen = chosen.reshape(chosen.shape + (1,) * (values.ndim - 2))
    spread_out = jnp.where(chosen[None], values[:, None], filler)
    return spread_out.reshape((values.shape[0] * stride,) + values.shape[1:])


def combine(levels):
    highest = levels[0][2]
    for one_level in levels[1:]:
        highest = jnp.maximum(highest, one_level[2])
    numerator = jnp.zeros(levels[0][0].shape, jnp.float32)
    denominator = jnp.zeros(levels[0][1].shape, jnp.float32)
    for one_level in levels:
        factor = jnp.exp(one_level[2] - highest)
        numerator = numerator + factor[:, :, None] * one_level[0]
        denominator = denominator + factor * one_level[1]
    return (numerator / denominator[:, :, None]).astype(jnp.bfloat16)


def reference(query, key, value, middle_offsets, upper_offsets, out_weight):
    query_matrix_rows = query.reshape(TOKENS, HEAD_TOTAL, HD)
    key_matrix_rows = key.reshape(TOKENS, HEAD_TOTAL, HD)
    value_matrix_rows = value.reshape(TOKENS, HEAD_TOTAL, HD)
    upper_result = attend_segment(picked_rows(query_matrix_rows, upper_offsets, TOP_DILATION), picked_rows(key_matrix_rows, upper_offsets, TOP_DILATION), picked_rows(value_matrix_rows, upper_offsets, TOP_DILATION))
    segment_length = SPAN * TOKENS_PER_SHARD
    upper_per_segment = segment_length // TOP_DILATION

    def one_segment(segment):
        row_begin = segment * segment_length
        segment_query = lax.dynamic_slice_in_dim(query_matrix_rows, row_begin, segment_length, 0)
        segment_key = lax.dynamic_slice_in_dim(key_matrix_rows, row_begin, segment_length, 0)
        segment_value = lax.dynamic_slice_in_dim(value_matrix_rows, row_begin, segment_length, 0)
        bottom = lax.map(attend_trio, (segment_query.reshape(SPAN, TOKENS_PER_SHARD, HEAD_TOTAL, HD), segment_key.reshape(SPAN, TOKENS_PER_SHARD, HEAD_TOTAL, HD), segment_value.reshape(SPAN, TOKENS_PER_SHARD, HEAD_TOTAL, HD)))
        bottom = (bottom[0].reshape(segment_length, HEAD_TOTAL, HD), bottom[1].reshape(segment_length, HEAD_TOTAL), bottom[2].reshape(segment_length, HEAD_TOTAL))
        middle_level = attend_segment(picked_rows(segment_query, middle_offsets, MIDDLE_DILATION), picked_rows(segment_key, middle_offsets, MIDDLE_DILATION), picked_rows(segment_value, middle_offsets, MIDDLE_DILATION))
        middle_level = (scatter_rows(middle_level[0], middle_offsets, MIDDLE_DILATION, 0.0), scatter_rows(middle_level[1], middle_offsets, MIDDLE_DILATION, 0.0), scatter_rows(middle_level[2], middle_offsets, MIDDLE_DILATION, -jnp.inf))
        top_start = segment * upper_per_segment
        upper_level = tuple(lax.dynamic_slice_in_dim(member, top_start, upper_per_segment, 0) for member in upper_result)
        upper_level = (scatter_rows(upper_level[0], upper_offsets, TOP_DILATION, 0.0), scatter_rows(upper_level[1], upper_offsets, TOP_DILATION, 0.0), scatter_rows(upper_level[2], upper_offsets, TOP_DILATION, -jnp.inf))
        attention = combine((bottom, middle_level, upper_level)).reshape(segment_length, HEAD_TOTAL * HD)
        return jnp.dot(attention, out_weight, preferred_element_type=jnp.float32).astype(jnp.bfloat16)

    outputs = lax.map(one_segment, jnp.arange(N_SEQ // SPAN, dtype=jnp.int32))
    return outputs.reshape(TOKENS, D)
```

```python
import functools

import jax
import jax.numpy as jnp
from jax import lax
from jax.experimental import pallas as pl
from jax.experimental.pallas import tpu as pltpu
from jax.sharding import PartitionSpec as P

HD = 64
SPAN = 8
MIDDLE_DILATION = 4


def partner_2(value, axis, stride):
    mask = 2**stride
    pairs = [(source, source ^ mask) for source in range(lax.axis_size(axis))]
    return lax.ppermute(value, axis, pairs)


def attend_segment(query_matrix_rows, key_matrix_rows, value_matrix_rows):
    scores = jnp.einsum(
        "qhd,khd->hqk", query_matrix_rows, key_matrix_rows, preferred_element_type=jnp.float32
    ) * HD ** (-0.5)
    row_max = jnp.max(scores, axis=2)
    mass = jnp.exp(scores - row_max[:, :, None])
    total = jnp.sum(mass, axis=2)
    soft_weights = mass.astype(jnp.bfloat16)
    weighted = jnp.einsum(
        "hqk,khd->qhd", soft_weights, value_matrix_rows, preferred_element_type=jnp.float32
    )
    return (weighted, total.T, row_max.T)


def attend_blocks(query_matrix_rows, key_matrix_rows, value_matrix_rows):
    block_size = min(512, query_matrix_rows.shape[0])
    pieces = query_matrix_rows.reshape(
        query_matrix_rows.shape[0] // block_size,
        block_size,
        query_matrix_rows.shape[1],
        query_matrix_rows.shape[2],
    )

    def one_block(one_piece):
        return attend_segment(one_piece, key_matrix_rows, value_matrix_rows)

    weighted, total, row_max = lax.map(one_block, pieces)
    return (
        weighted.reshape(query_matrix_rows.shape),
        total.reshape(query_matrix_rows.shape[:2]),
        row_max.reshape(query_matrix_rows.shape[:2]),
    )


def picked_rows(block_rows, offsets, stride):
    group_count = block_rows.shape[0] // stride
    grouped = block_rows.reshape(group_count, stride, block_rows.shape[1], block_rows.shape[2])
    chosen = (
        jnp.arange(stride, dtype=jnp.int32)[None, :, None, None] == offsets[None, None, :, None]
    )
    return jnp.sum(jnp.where(chosen, grouped, jnp.zeros((), grouped.dtype)), axis=1)


def scatter_rows(values, offsets, stride, filler):
    chosen = jnp.arange(stride, dtype=jnp.int32)[:, None] == offsets[None, :]
    spread_out = jnp.where(chosen[None], values[:, None], filler)
    return spread_out.reshape((values.shape[0] * stride,) + values.shape[1:])


def flatten_level(result):
    row_total = result[0].shape[0]
    weighted = result[0].reshape(row_total, -1)
    total = jnp.repeat(result[1], HD, axis=1)
    row_max = jnp.repeat(result[2], HD, axis=1)
    return (weighted, total, row_max)


def scatter_level(result, offsets, stride):
    weighted, total, row_max = flatten_level(result)
    column_offsets = jnp.repeat(offsets, HD)
    return (
        scatter_rows(weighted, column_offsets, stride, 0.0),
        scatter_rows(total, column_offsets, stride, 0.0),
        scatter_rows(row_max, column_offsets, stride, -jnp.inf),
    )


def combine(levels):
    highest = levels[0][2]
    for one_level in levels[1:]:
        highest = jnp.maximum(highest, one_level[2])
    numerator = jnp.zeros(levels[0][0].shape, jnp.float32)
    denominator = jnp.zeros(levels[0][1].shape, jnp.float32)
    for one_level in levels:
        factor = jnp.exp(one_level[2] - highest)
        numerator = numerator + factor * one_level[0]
        denominator = denominator + factor * one_level[1]
    return (numerator / denominator).astype(jnp.bfloat16)


def per_device(query, key, value, middle_offsets, upper_offsets, out_weight):
    row_count = query.shape[0]
    head_count = query.shape[1] // HD
    top_stride = lax.axis_size("seq") // 2
    query_matrix_rows = query.reshape(row_count, head_count, HD)
    key_matrix_rows = key.reshape(row_count, head_count, HD)
    value_matrix_rows = value.reshape(row_count, head_count, HD)
    top_key_local = picked_rows(key_matrix_rows, upper_offsets, top_stride).reshape(
        -1, head_count * HD
    )
    top_value_local = picked_rows(value_matrix_rows, upper_offsets, top_stride).reshape(
        -1, head_count * HD
    )
    top_key_all, top_value_all = (
        lax.all_gather(top_key_local, "seq", axis=0, tiled=True),
        lax.all_gather(top_value_local, "seq", axis=0, tiled=True),
    )
    upper_level = attend_segment(
        picked_rows(query_matrix_rows, upper_offsets, top_stride),
        top_key_all.reshape(-1, head_count, HD),
        top_value_all.reshape(-1, head_count, HD),
    )
    middle_pair = jnp.stack(
        [
            picked_rows(key_matrix_rows, middle_offsets, MIDDLE_DILATION),
            picked_rows(value_matrix_rows, middle_offsets, MIDDLE_DILATION),
        ]
    ).reshape(2, -1, head_count * HD)
    for bit_number in range(SPAN.bit_length() - 1):
        partner = partner_2(middle_pair, "seq", bit_number)
        middle_pair = jnp.concatenate([middle_pair, partner], axis=1)
    middle_level = attend_segment(
        picked_rows(query_matrix_rows, middle_offsets, MIDDLE_DILATION),
        middle_pair[0].reshape(-1, head_count, HD),
        middle_pair[1].reshape(-1, head_count, HD),
    )
    bottom = flatten_level(attend_blocks(query_matrix_rows, key_matrix_rows, value_matrix_rows))
    attention = combine(
        (
            bottom,
            scatter_level(middle_level, middle_offsets, MIDDLE_DILATION),
            scatter_level(upper_level, upper_offsets, top_stride),
        )
    )
    summed = lax.psum_scatter(
        jnp.dot(attention, out_weight, preferred_element_type=jnp.float32),
        "head",
        scatter_dimension=0,
        tiled=True,
    )
    return summed.astype(jnp.bfloat16)


MESH = pl.DeviceIdType.MESH
SHARED_ROWS = 96


def dot_f32(left, right):
    return jnp.dot(left, right, preferred_element_type=jnp.float32)


def three_parts(value):
    high = value.astype(jnp.bfloat16).astype(jnp.float32)
    rest = value - high
    middle = rest.astype(jnp.bfloat16).astype(jnp.float32)
    return [high, middle, rest - middle]


def fused_kernel(
    seq_total,
    query_hbm,
    key_hbm,
    value_hbm,
    middle_hbm,
    upper_hbm,
    weight_hbm,
    out_ref,
    query_ref,
    key_ref,
    value_ref,
    middle_ref,
    upper_ref,
    load,
    sent_kv,
    sent_q,
    got_kv,
    got_q,
    result,
    result_stat,
    returned,
    returned_stat,
    bottom,
    bottom_stat,
    bottom_got,
    bottom_stat_got,
    weights,
    attention,
    send_kv,
    recv_kv,
    send_q,
    recv_q,
    send_back,
    recv_back,
    send_stat,
    recv_stat,
    send_bottom,
    recv_bottom,
    send_weight,
    recv_weight,
):
    seq, head = lax.axis_index("seq"), lax.axis_index("head")
    chip, core = lax.div(head, 2), lax.rem(head, 2)
    beside_head = 2 * chip + (1 - core)
    across_head = 2 * (1 - chip) + core
    y = lax.rem(seq, 2)
    y_peer = seq + 1 - 2 * y
    rows = query_ref.shape[0]
    heads = query_ref.shape[1] // HD
    taken = rows // MIDDLE_DILATION
    part = taken // 4
    half_total = seq_total // 2
    offset_refs = (middle_ref, upper_ref)
    my_half, my_low = lax.div(seq, half_total), lax.rem(seq, half_total)

    def target_of(slot):
        half = lax.rem(my_half + slot // half_total, 2)
        return half * half_total + lax.rem(my_low + slot % half_total, half_total)

    def source_of(slot):
        half = lax.rem(my_half + slot // half_total, 2)
        return half * half_total + lax.rem(
            my_low + half_total - slot % half_total, half_total
        )

    loads = []
    for i, (source, target) in enumerate(
        (
            (middle_hbm, middle_ref),
            (upper_hbm, upper_ref),
            (query_hbm, query_ref),
            (value_hbm, value_ref),
            (key_hbm, key_ref),
            (weight_hbm, weights.at[head]),
        )
    ):
        loads.append(pltpu.make_async_copy(source, target, load.at[i]))
        loads[-1].start()

    barrier = pltpu.get_barrier_semaphore()
    for step in range(1, seq_total):
        pl.semaphore_signal(
            barrier,
            inc=1,
            device_id=(lax.rem(seq + step, seq_total), head),
            device_id_type=MESH,
        )
    for step in range(1, 4):
        pl.semaphore_signal(
            barrier, inc=1, device_id=(seq, lax.rem(head + step, 4)), device_id_type=MESH
        )

    for copy in loads[:5]:
        copy.wait()
    query_t = (query_ref[...] * jnp.bfloat16(HD**-0.5)).T
    value_t = value_ref[...].T
    distance = lax.broadcasted_iota(jnp.int32, (taken, rows), 1) - MIDDLE_DILATION * (
        lax.broadcasted_iota(jnp.int32, (taken, rows), 0)
    )
    for one in range(heads):
        span = slice(one * HD, (one + 1) * HD)
        both_t = jnp.concatenate([value_t[span], query_t[span]], axis=0)
        for level in range(2):
            pair = level * heads + one
            chosen = jnp.where(
                distance == offset_refs[level][one], jnp.float32(1), jnp.float32(0)
            ).astype(jnp.bfloat16)
            picked_t = lax.dot_general(
                both_t,
                chosen,
                (((1,), (1,)), ((), ())),
                preferred_element_type=jnp.float32,
            ).astype(jnp.bfloat16)
            sent_kv[pair, 0:HD] = picked_t[0:HD]
            sent_q[pair] = picked_t[HD : 2 * HD]
            picked = dot_f32(chosen, key_ref[:, span])
            sent_kv[pair, HD : 2 * HD] = jnp.concatenate(
                [picked[: taken // 2], picked[taken // 2 :]], axis=1
            ).astype(jnp.bfloat16)

    pl.semaphore_wait(barrier, seq_total + 2)
    waits = []

    def send(source, target, send_sem, recv_sem, device):
        copy = pltpu.make_async_remote_copy(
            src_ref=source,
            dst_ref=target,
            send_sem=send_sem,
            recv_sem=recv_sem,
            device_id=device,
            device_id_type=MESH,
        )
        copy.start()
        return copy

    near = list(range(1, half_total))
    far = list(range(half_total, seq_total))
    for slot in KV_ORDER:
        to = target_of(slot)
        waits.append(
            send(sent_kv.at[to], got_kv.at[seq], send_kv.at[slot], recv_kv, (to, head))
        )
    for slot in Q_ORDER:
        to = target_of(slot)
        waits.append(
            send(sent_q.at[to], got_q.at[slot], send_q.at[slot], recv_q.at[slot], (to, head))
        )
    got_kv[seq] = sent_kv[seq]
    got_q[0] = sent_q[seq]

    loads[5].wait()
    own_rows = weights.shape[1]
    middle_rows = own_rows - 2 * SHARED_ROWS
    mine = pl.ds(y * (own_rows - SHARED_ROWS), SHARED_ROWS)
    others = pl.ds((1 - y) * (own_rows - SHARED_ROWS), SHARED_ROWS)
    common = pl.ds(SHARED_ROWS, middle_rows)

    def send_weight_rows(which, part_rows, index, device):
        block = weights.at[which, part_rows]
        copy = send(block, block, send_weight.at[index], recv_weight.at[index], device)
        waits.append(copy)
        return copy

    def weight_arrived(which, part_rows, index):
        block = weights.at[which, part_rows]
        pltpu.make_async_copy(block, block, recv_weight.at[index]).wait()

    send_weight_rows(head, mine, 0, (seq, across_head))
    send_weight_rows(head, common, 1, (seq, across_head))
    send_weight_rows(head, pl.ds(0, own_rows), 3, (seq, beside_head))

    residue = lax.rem(lax.broadcasted_iota(jnp.int32, (1, taken), 1), MIDDLE_DILATION)
    half = rows // 2
    blocks = half // taken
    for one in range(heads):
        span = slice(one * HD, (one + 1) * HD)
        for piece in range(2):
            lanes = slice(piece * half, (piece + 1) * half)
            scores = dot_f32(key_ref[:, span], query_t[span, lanes])
            row_max = jnp.max(scores, axis=0, keepdims=True)
            mass = jnp.exp(scores - row_max)
            total = jnp.sum(mass, axis=0, keepdims=True)
            weighted = dot_f32(value_t[span], mass.astype(jnp.bfloat16))
            weighted = (weighted * (1.0 / total)).astype(jnp.bfloat16)
            logs = row_max + jnp.log(total)
            for i in range(blocks):
                cut = slice(i * taken, (i + 1) * taken)
                bottom[piece * blocks + i, span] = weighted[:, cut]
                bottom_stat[piece * blocks + i, one : one + 1] = logs[:, cut]
        for level in range(2):
            bias = jnp.where(residue == offset_refs[level][one], 0.0, -jnp.inf)
            row = (level + 1) * heads + one
            for i in range(4):
                bottom_stat[i, row : row + 1] = bias
    for i in range(4):
        bottom_stat[i, 3 * heads :] = jnp.zeros((heads, taken), jnp.float32)

    for step in range(1, 4):
        to = lax.rem(head + step, 4)
        waits.append(
            send(
                bottom.at[to],
                bottom_got.at[head],
                send_bottom.at[step],
                recv_bottom.at[0],
                (seq, to),
            )
        )
        waits.append(
            send(
                bottom_stat.at[to],
                bottom_stat_got.at[head],
                send_bottom.at[4 + step],
                recv_bottom.at[1],
                (seq, to),
            )
        )
    bottom_got[head] = bottom[head]
    bottom_stat_got[head] = bottom_stat[head]

    weight_arrived(across_head, mine, 0)
    send_weight_rows(across_head, mine, 2, (y_peer, head))
    send_weight_rows(across_head, mine, 4, (seq, beside_head))

    def arrived(ref, count, sem):
        block = ref.at[pl.ds(0, count)]
        pltpu.make_async_copy(block, block, sem).wait()

    arrived(got_kv, seq_total - 1, recv_kv)
    keys = jnp.concatenate([got_kv[i, HD : 2 * HD] for i in range(seq_total)], axis=0)
    values_t = jnp.concatenate([got_kv[i, 0:HD] for i in range(seq_total)], axis=1)
    place = lax.div(seq, heads) * (4 * heads) + head * heads + lax.rem(seq, heads)
    for slots in BLOCKS:
        for slot in slots:
            if slot != 0:
                block = got_q.at[slot]
                pltpu.make_async_copy(block, block, recv_q.at[slot]).wait()
        block = jnp.concatenate([got_q[slot] for slot in slots], axis=1)
        blank = jnp.zeros_like(block)
        first = dot_f32(keys, jnp.concatenate([block, blank], axis=0))
        second = dot_f32(keys, jnp.concatenate([blank, block], axis=0))
        row_max = jnp.maximum(
            jnp.max(first, axis=0, keepdims=True), jnp.max(second, axis=0, keepdims=True)
        )
        first = jnp.exp(first - row_max)
        second = jnp.exp(second - row_max)
        total = jnp.sum(first, axis=0, keepdims=True) + jnp.sum(
            second, axis=0, keepdims=True
        )
        first = first.astype(jnp.bfloat16)
        second = second.astype(jnp.bfloat16)
        pieces = []
        for i in range(seq_total):
            pieces.append(first[i * HD : (i + 1) * HD])
            pieces.append(second[i * HD : (i + 1) * HD])
        weighted = dot_f32(values_t, jnp.concatenate(pieces, axis=0))
        weighted = weighted * (1.0 / total)
        logs = row_max + jnp.log(total)
        for slot, begin in zip(slots, range(0, len(slots) * taken, taken)):
            for i in range(4):
                lanes = slice(begin + i * part, begin + (i + 1) * part)
                result[slot, i] = jnp.concatenate(
                    [weighted[16 * c : 16 * (c + 1), lanes] for c in range(4)], axis=1
                ).astype(jnp.bfloat16)
            result_stat[slot] = logs[:, begin : begin + taken]
            to = source_of(slot)
            for step in range(0 if slot else 1, 4):
                i = lax.rem(head + step, 4)
                waits.append(
                    send(
                        result.at[slot, i],
                        returned.at[place],
                        send_back.at[slot, step],
                        recv_back,
                        (to, i),
                    )
                )
                waits.append(
                    send(
                        result_stat.at[slot],
                        returned_stat.at[place],
                        send_stat.at[slot, step],
                        recv_stat,
                        (to, i),
                    )
                )
            if slot == 0:
                returned[place] = result[0, head]
                returned_stat[place] = result_stat[0]

    weight_arrived(across_head, common, 1)
    send_weight_rows(across_head, common, 5, (seq, beside_head))
    weight_arrived(across_head, others, 2)
    send_weight_rows(across_head, others, 6, (seq, beside_head))

    repeat = (
        (
            lax.broadcasted_iota(jnp.int32, (taken, rows), 0)
            == part * (lax.broadcasted_iota(jnp.int32, (taken, rows), 1) // taken)
            + (lax.broadcasted_iota(jnp.int32, (taken, rows), 1) % taken) // MIDDLE_DILATION
        )
        .astype(jnp.float32)
        .astype(jnp.bfloat16)
    )
    repeat_stat = (
        (
            lax.broadcasted_iota(jnp.int32, (taken, taken), 0)
            == part * head + lax.broadcasted_iota(jnp.int32, (taken, taken), 1) // MIDDLE_DILATION
        )
        .astype(jnp.float32)
        .astype(jnp.bfloat16)
    )
    arrived(bottom_got, 3, recv_bottom.at[0])
    arrived(bottom_stat_got, 3, recv_bottom.at[1])
    pairs = returned.shape[0]
    arrived(returned_stat, pairs - 1, recv_stat)
    logs = sum(
        dot_f32(value.astype(jnp.bfloat16), repeat_stat)
        for value in three_parts(returned_stat[...].reshape(pairs, taken))
    )

    def stat_rows(begin):
        return jnp.concatenate(
            [bottom_stat_got[i, begin : begin + heads] for i in range(4)], axis=0
        )

    all_logs = [stat_rows(0)]
    for level in range(2):
        level_logs = logs[level * 4 * heads : (level + 1) * 4 * heads]
        all_logs.append(level_logs + stat_rows((level + 1) * heads))
    highest = jnp.maximum(jnp.maximum(all_logs[0], all_logs[1]), all_logs[2])
    factors = [jnp.exp(one_log - highest) for one_log in all_logs]
    inverse = 1.0 / (factors[0] + factors[1] + factors[2])
    factors = [factor * inverse for factor in factors]

    arrived(returned, pairs - 1, recv_back)
    spread = dot_f32(returned[...].reshape(pairs * 16, taken), repeat)
    for one in range(4 * heads):
        for c in range(4):
            lanes = slice(c * taken, (c + 1) * taken)
            begin = (one % heads) * HD + 16 * c
            total = factors[0][one : one + 1] * bottom_got[
                one // heads, begin : begin + 16
            ].astype(jnp.float32)
            for level in range(2):
                at = (level * 4 * heads + one) * 16
                total += factors[level + 1][one : one + 1] * spread[at : at + 16, lanes]
            attention[one * HD + 16 * c : one * HD + 16 * (c + 1)] = total.astype(
                jnp.bfloat16
            )

    weight_arrived(beside_head, pl.ds(0, own_rows), 3)
    diagonal = 2 * (1 - chip) + (1 - core)
    weight_arrived(diagonal, mine, 4)
    weight_arrived(diagonal, common, 5)
    weight_arrived(diagonal, others, 6)
    projected = dot_f32(attention[0:own_rows].T, weights[0])
    for i in range(1, 4):
        projected += dot_f32(attention[i * own_rows : (i + 1) * own_rows].T, weights[i])
    out_ref[...] = projected.astype(out_ref.dtype)
    for copy in waits:
        copy.wait_send()


KV_ORDER = (4, 1, 5, 2, 6, 3, 7)
Q_ORDER = (4, 5, 6, 7, 1, 2, 3)
BLOCKS = ((4, 5), (6, 7), (1, 2), (3, 0))


def per_device_fused(query, key, value, middle_offsets, upper_offsets, out_weight):
    rows, width = query.shape
    seq_total = lax.axis_size("seq")
    heads = width // HD
    pairs = 2 * heads
    taken = rows // MIDDLE_DILATION
    anywhere = pl.BlockSpec(memory_space=pl.ANY)
    dma = pltpu.SemaphoreType.DMA
    bf16, f32 = jnp.bfloat16, jnp.float32
    return pl.pallas_call(
        functools.partial(fused_kernel, seq_total),
        out_shape=pltpu.VMEM((rows // 4, out_weight.shape[1]), bf16),
        in_specs=[anywhere] * 6,
        out_specs=pl.BlockSpec(memory_space=pltpu.VMEM),
        scratch_shapes=[
            pltpu.VMEM(query.shape, query.dtype),
            pltpu.VMEM(key.shape, key.dtype),
            pltpu.VMEM(value.shape, value.dtype),
            pltpu.SMEM(middle_offsets.shape, jnp.int32),
            pltpu.SMEM(upper_offsets.shape, jnp.int32),
            dma((6,)),
            pltpu.VMEM((pairs, 2 * HD, taken), bf16),
            pltpu.VMEM((pairs, HD, taken), bf16),
            pltpu.VMEM((seq_total, 2 * HD, taken), bf16),
            pltpu.VMEM((seq_total, HD, taken), bf16),
            pltpu.VMEM((seq_total, 4, 16, taken), bf16),
            pltpu.VMEM((seq_total, 1, taken), f32),
            pltpu.VMEM((4 * pairs, 16, taken), bf16),
            pltpu.VMEM((4 * pairs, 1, taken), f32),
            pltpu.VMEM((4, width, taken), bf16),
            pltpu.VMEM((4, 4 * heads, taken), f32),
            pltpu.VMEM((4, width, taken), bf16),
            pltpu.VMEM((4, 4 * heads, taken), f32),
            pltpu.VMEM((4,) + out_weight.shape, bf16),
            pltpu.VMEM((4 * width, taken), bf16),
            dma((seq_total,)),
            dma,
            dma((seq_total,)),
            dma((seq_total,)),
            dma((seq_total, 4)),
            dma,
            dma((seq_total, 4)),
            dma,
            dma((8,)),
            dma((2,)),
            dma((7,)),
            dma((7,)),
        ],
        compiler_params=pltpu.CompilerParams(
            collective_id=0, has_side_effects=True, vmem_limit_bytes=56 * 2**20
        ),
    )(query, key, value, middle_offsets, upper_offsets, out_weight)


def solution(mesh):
    in_specs = (
        P("seq", "head"),
        P("seq", "head"),
        P("seq", "head"),
        P("head"),
        P("head"),
        P("head", None),
    )
    out_specs = P(("seq", "head"), None)
    seq_total, head_shards = mesh.shape["seq"], mesh.shape["head"]
    one_segment = seq_total == SPAN and seq_total // 2 == MIDDLE_DILATION and head_shards == 4
    return jax.shard_map(
        per_device_fused if one_segment else per_device, mesh=mesh, in_specs=in_specs, out_specs=out_specs, check_vma=False
    )
```

```python
import functools

import jax
import jax.numpy as jnp
from jax import lax
from jax.experimental import pallas as pl
from jax.experimental.pallas import tpu as pltpu
from jax.sharding import PartitionSpec as P

HD = 64
SPAN = 8
MIDDLE_DILATION = 4


def partner_2(value, axis, stride):
    mask = 2**stride
    pairs = [(source, source ^ mask) for source in range(lax.axis_size(axis))]
    return lax.ppermute(value, axis, pairs)


def attend_segment(query_matrix_rows, key_matrix_rows, value_matrix_rows):
    scores = jnp.einsum(
        "qhd,khd->hqk", query_matrix_rows, key_matrix_rows, preferred_element_type=jnp.float32
    ) * HD ** (-0.5)
    row_max = jnp.max(scores, axis=2)
    mass = jnp.exp(scores - row_max[:, :, None])
    total = jnp.sum(mass, axis=2)
    soft_weights = mass.astype(jnp.bfloat16)
    weighted = jnp.einsum(
        "hqk,khd->qhd", soft_weights, value_matrix_rows, preferred_element_type=jnp.float32
    )
    return (weighted, total.T, row_max.T)


def attend_blocks(query_matrix_rows, key_matrix_rows, value_matrix_rows):
    block_size = min(512, query_matrix_rows.shape[0])
    pieces = query_matrix_rows.reshape(
        query_matrix_rows.shape[0] // block_size,
        block_size,
        query_matrix_rows.shape[1],
        query_matrix_rows.shape[2],
    )

    def one_block(one_piece):
        return attend_segment(one_piece, key_matrix_rows, value_matrix_rows)

    weighted, total, row_max = lax.map(one_block, pieces)
    return (
        weighted.reshape(query_matrix_rows.shape),
        total.reshape(query_matrix_rows.shape[:2]),
        row_max.reshape(query_matrix_rows.shape[:2]),
    )


def picked_rows(block_rows, offsets, stride):
    group_count = block_rows.shape[0] // stride
    grouped = block_rows.reshape(group_count, stride, block_rows.shape[1], block_rows.shape[2])
    chosen = (
        jnp.arange(stride, dtype=jnp.int32)[None, :, None, None] == offsets[None, None, :, None]
    )
    return jnp.sum(jnp.where(chosen, grouped, jnp.zeros((), grouped.dtype)), axis=1)


def scatter_rows(values, offsets, stride, filler):
    chosen = jnp.arange(stride, dtype=jnp.int32)[:, None] == offsets[None, :]
    spread_out = jnp.where(chosen[None], values[:, None], filler)
    return spread_out.reshape((values.shape[0] * stride,) + values.shape[1:])


def flatten_level(result):
    row_total = result[0].shape[0]
    weighted = result[0].reshape(row_total, -1)
    total = jnp.repeat(result[1], HD, axis=1)
    row_max = jnp.repeat(result[2], HD, axis=1)
    return (weighted, total, row_max)


def scatter_level(result, offsets, stride):
    weighted, total, row_max = flatten_level(result)
    column_offsets = jnp.repeat(offsets, HD)
    return (
        scatter_rows(weighted, column_offsets, stride, 0.0),
        scatter_rows(total, column_offsets, stride, 0.0),
        scatter_rows(row_max, column_offsets, stride, -jnp.inf),
    )


def combine(levels):
    highest = levels[0][2]
    for one_level in levels[1:]:
        highest = jnp.maximum(highest, one_level[2])
    numerator = jnp.zeros(levels[0][0].shape, jnp.float32)
    denominator = jnp.zeros(levels[0][1].shape, jnp.float32)
    for one_level in levels:
        factor = jnp.exp(one_level[2] - highest)
        numerator = numerator + factor * one_level[0]
        denominator = denominator + factor * one_level[1]
    return (numerator / denominator).astype(jnp.bfloat16)


def per_device(query, key, value, middle_offsets, upper_offsets, out_weight):
    row_count = query.shape[0]
    head_count = query.shape[1] // HD
    top_stride = lax.axis_size("seq") // 2
    query_matrix_rows = query.reshape(row_count, head_count, HD)
    key_matrix_rows = key.reshape(row_count, head_count, HD)
    value_matrix_rows = value.reshape(row_count, head_count, HD)
    top_key_local = picked_rows(key_matrix_rows, upper_offsets, top_stride).reshape(
        -1, head_count * HD
    )
    top_value_local = picked_rows(value_matrix_rows, upper_offsets, top_stride).reshape(
        -1, head_count * HD
    )
    top_key_all, top_value_all = (
        lax.all_gather(top_key_local, "seq", axis=0, tiled=True),
        lax.all_gather(top_value_local, "seq", axis=0, tiled=True),
    )
    upper_level = attend_segment(
        picked_rows(query_matrix_rows, upper_offsets, top_stride),
        top_key_all.reshape(-1, head_count, HD),
        top_value_all.reshape(-1, head_count, HD),
    )
    middle_pair = jnp.stack(
        [
            picked_rows(key_matrix_rows, middle_offsets, MIDDLE_DILATION),
            picked_rows(value_matrix_rows, middle_offsets, MIDDLE_DILATION),
        ]
    ).reshape(2, -1, head_count * HD)
    for bit_number in range(SPAN.bit_length() - 1):
        partner = partner_2(middle_pair, "seq", bit_number)
        middle_pair = jnp.concatenate([middle_pair, partner], axis=1)
    middle_level = attend_segment(
        picked_rows(query_matrix_rows, middle_offsets, MIDDLE_DILATION),
        middle_pair[0].reshape(-1, head_count, HD),
        middle_pair[1].reshape(-1, head_count, HD),
    )
    bottom = flatten_level(attend_blocks(query_matrix_rows, key_matrix_rows, value_matrix_rows))
    attention = combine(
        (
            bottom,
            scatter_level(middle_level, middle_offsets, MIDDLE_DILATION),
            scatter_level(upper_level, upper_offsets, top_stride),
        )
    )
    summed = lax.psum_scatter(
        jnp.dot(attention, out_weight, preferred_element_type=jnp.float32),
        "head",
        scatter_dimension=0,
        tiled=True,
    )
    return summed.astype(jnp.bfloat16)


MESH = pl.DeviceIdType.MESH
SHARED_ROWS = 96


def dot_f32(left, right):
    return jnp.dot(left, right, preferred_element_type=jnp.float32)


def three_parts(value):
    high = value.astype(jnp.bfloat16).astype(jnp.float32)
    rest = value - high
    middle = rest.astype(jnp.bfloat16).astype(jnp.float32)
    return [high, middle, rest - middle]


def softmax_of(scores):
    row_max = jnp.max(scores, axis=0, keepdims=True)
    return row_max, jnp.exp(scores - row_max).astype(jnp.bfloat16)


def weigh(values_with_ones, row_max, mass):
    summed = dot_f32(values_with_ones, mass)
    total = summed[HD : HD + 1]
    weighted = (summed[:HD] * (1.0 / total)).astype(jnp.bfloat16)
    return weighted, row_max + jnp.log(total)


def with_ones(values_t):
    ones = jnp.ones((16, values_t.shape[1]), values_t.dtype)
    return jnp.concatenate([values_t, ones], axis=0)


def pipelined(units, ahead, lag):
    scores, masses = {}, {}
    for i in range(len(units) + ahead + lag):
        if i < len(units):
            scores[i] = units[i][0]()
        j = i - ahead
        if 0 <= j < len(units):
            soften = units[j][2] if len(units[j]) > 2 else softmax_of
            masses[j] = soften(scores.pop(j))
        k = j - lag
        if 0 <= k < len(units):
            units[k][1](*masses.pop(k))


def select_half(block, which):
    blank = jnp.zeros_like(block)
    return jnp.concatenate([blank, block] if which else [block, blank], axis=0)


def fused_kernel(
    seq_total,
    query_hbm,
    key_hbm,
    value_hbm,
    middle_hbm,
    upper_hbm,
    weight_hbm,
    out_ref,
    query_ref,
    key_ref,
    value_ref,
    middle_ref,
    upper_ref,
    load,
    sent_kv,
    sent_q,
    got_kv,
    got_q,
    result,
    result_stat,
    returned,
    returned_stat,
    bottom,
    bottom_stat,
    bottom_got,
    bottom_stat_got,
    weights,
    attention,
    send_kv,
    recv_kv,
    send_q,
    recv_q,
    send_back,
    recv_back,
    send_stat,
    recv_stat,
    send_bottom,
    recv_bottom,
    send_weight,
    recv_weight,
):
    seq, head = lax.axis_index("seq"), lax.axis_index("head")
    chip, core = lax.div(head, 2), lax.rem(head, 2)
    beside_head = 2 * chip + (1 - core)
    across_head = 2 * (1 - chip) + core
    y = lax.rem(seq, 2)
    y_peer = seq + 1 - 2 * y
    rows = query_ref.shape[0]
    heads = query_ref.shape[1] // HD
    taken = rows // MIDDLE_DILATION
    part = taken // 4
    half_total = seq_total // 2
    offset_refs = (middle_ref, upper_ref)
    my_half, my_low = lax.div(seq, half_total), lax.rem(seq, half_total)
    my_inner = lax.rem(lax.div(seq, 2) + my_half, 2)

    def target_of(slot):
        half = lax.rem(my_half + slot // half_total, 2)
        return half * half_total + lax.rem(my_low + slot % half_total, half_total)

    z = lax.div(seq, 2)
    my_inner = lax.rem(z + my_half, 2)

    barrier = pltpu.get_barrier_semaphore()
    for step in range(1, seq_total):
        pl.semaphore_signal(
            barrier,
            inc=1,
            device_id=(lax.rem(seq + step, seq_total), head),
            device_id_type=MESH,
        )
    for step in range(1, 4):
        pl.semaphore_signal(
            barrier, inc=1, device_id=(seq, lax.rem(head + step, 4)), device_id_type=MESH
        )

    loads = []
    for i, (source, target) in enumerate(
        (
            (middle_hbm, middle_ref),
            (upper_hbm, upper_ref),
            (key_hbm, key_ref),
            (value_hbm, value_ref),
            (query_hbm, query_ref),
            (weight_hbm, weights.at[head]),
        )
    ):
        loads.append(pltpu.make_async_copy(source, target, load.at[i]))
    for copy in loads[:5]:
        copy.start()
    distance = lax.broadcasted_iota(jnp.int32, (taken, rows), 1) - MIDDLE_DILATION * (
        lax.broadcasted_iota(jnp.int32, (taken, rows), 0)
    )

    def pick(source_t, one, chosen):
        return lax.dot_general(
            source_t[one * HD : (one + 1) * HD],
            chosen,
            (((1,), (1,)), ((), ())),
            preferred_element_type=jnp.float32,
        ).astype(jnp.bfloat16)

    for copy in loads[:4]:
        copy.wait()
    value_t = value_ref[...].T
    select = {}
    for one in range(heads):
        for level in range(2):
            pair = level * heads + one
            chosen = jnp.where(
                distance == offset_refs[level][one], jnp.float32(1), jnp.float32(0)
            ).astype(jnp.bfloat16)
            select[pair] = chosen
            sent_kv[pair, 0:HD] = pick(value_t, one, chosen)
            picked = dot_f32(chosen, key_ref[:, one * HD : (one + 1) * HD])
            sent_kv[pair, HD : 2 * HD] = jnp.concatenate(
                [picked[: taken // 2], picked[taken // 2 :]], axis=1
            ).astype(jnp.bfloat16)

    pl.semaphore_wait(barrier, seq_total + 2)
    waits = []

    def send(source, target, send_sem, recv_sem, device):
        copy = pltpu.make_async_remote_copy(
            src_ref=source,
            dst_ref=target,
            send_sem=send_sem,
            recv_sem=recv_sem,
            device_id=device,
            device_id_type=MESH,
        )
        copy.start()
        return copy

    def send_kv_to(slot):
        to = target_of(slot)
        sem = recv_kv.at[my_inner] if slot >= half_total else recv_kv.at[2]
        waits.append(
            send(sent_kv.at[to], got_kv.at[seq], send_kv.at[slot], sem, (to, head))
        )

    def send_q_to(slot):
        to = target_of(slot)
        copy = pltpu.make_async_remote_copy(
            src_ref=sent_q.at[to],
            dst_ref=got_q.at[seq],
            send_sem=send_q.at[slot],
            recv_sem=recv_q.at[seq],
            device_id=(to, head),
            device_id_type=MESH,
        )
        copy.start()

    for slot in KV_ORDER:
        send_kv_to(slot)
    loads[5].start()
    loads[4].wait()
    query_t = (query_ref[...] * jnp.bfloat16(HD**-0.5)).T
    for one in range(heads):
        for level in range(2):
            pair = level * heads + one
            sent_q[pair] = pick(query_t, one, select[pair])
    got_kv[seq] = sent_kv[seq]
    own_q = pltpu.make_async_copy(sent_q.at[seq], got_q.at[seq], recv_q.at[seq])
    own_q.start()
    for slot in range(1, half_total):
        send_q_to(slot)

    def send_far_q():
        for slot in range(half_total, seq_total):
            send_q_to(slot)

    pl.when(my_half < GATED_HALVES)(send_far_q)
    loads[5].wait()
    own_rows = weights.shape[1]
    middle_rows = own_rows - 2 * SHARED_ROWS
    mine = pl.ds(y * (own_rows - SHARED_ROWS), SHARED_ROWS)
    others = pl.ds((1 - y) * (own_rows - SHARED_ROWS), SHARED_ROWS)
    common = pl.ds(SHARED_ROWS, middle_rows)

    def send_weight_rows(which, part_rows, index, device):
        block = weights.at[which, part_rows]
        copy = send(block, block, send_weight.at[index], recv_weight.at[index], device)
        waits.append(copy)
        return copy

    def weight_arrived(which, part_rows, index):
        block = weights.at[which, part_rows]
        pltpu.make_async_copy(block, block, recv_weight.at[index]).wait()

    send_weight_rows(head, mine, 0, (seq, across_head))
    send_weight_rows(head, common, 1, (seq, across_head))
    send_weight_rows(head, pl.ds(0, own_rows), 3, (seq, beside_head))

    residue = lax.rem(lax.broadcasted_iota(jnp.int32, (1, taken), 1), MIDDLE_DILATION)
    half = rows // 2
    blocks = half // taken
    units = []
    for one in range(heads):
        for piece in range(2):

            def bottom_scores(one=one, piece=piece):
                both = slice(one // 2 * 2 * HD, (one // 2 + 1) * 2 * HD)
                block = query_t[one * HD : (one + 1) * HD, piece * half : (piece + 1) * half]
                return dot_f32(key_ref[:, both], select_half(block, one % 2))

            def bottom_sums(row_max, mass, one=one, piece=piece):
                span = slice(one * HD, (one + 1) * HD)
                weighted, logs = weigh(with_ones(value_t[span]), row_max, mass)
                for i in range(blocks):
                    cut = slice(i * taken, (i + 1) * taken)
                    bottom[piece * blocks + i, span] = weighted[:, cut]
                    bottom_stat[piece * blocks + i, one : one + 1] = logs[:, cut]

            units.append((bottom_scores, bottom_sums))
    pipelined(units, 2, 1)
    for one in range(heads):
        for level in range(2):
            bias = jnp.where(residue == offset_refs[level][one], 0.0, -jnp.inf)
            row = (level + 1) * heads + one
            for i in range(4):
                bottom_stat[i, row : row + 1] = bias
    for i in range(4):
        bottom_stat[i, 3 * heads :] = jnp.zeros((heads, taken), jnp.float32)

    for step in range(1, 4):
        to = lax.rem(head + step, 4)
        waits.append(
            send(
                bottom.at[to],
                bottom_got.at[head],
                send_bottom.at[step],
                recv_bottom.at[0],
                (seq, to),
            )
        )
        waits.append(
            send(
                bottom_stat.at[to],
                bottom_stat_got.at[head],
                send_bottom.at[4 + step],
                recv_bottom.at[1],
                (seq, to),
            )
        )
    bottom_got[head] = bottom[head]
    bottom_stat_got[head] = bottom_stat[head]

    def arrived(ref, count, sem):
        block = ref.at[pl.ds(0, count)]
        pltpu.make_async_copy(block, block, sem).wait()

    arrived(got_kv, 2, recv_kv.at[0])
    pl.when(my_half >= GATED_HALVES)(send_far_q)

    weight_arrived(across_head, mine, 0)
    send_weight_rows(across_head, mine, 2, (y_peer, head))
    send_weight_rows(across_head, mine, 4, (seq, beside_head))

    arrived(got_kv, 2, recv_kv.at[1])
    arrived(got_kv, half_total - 1, recv_kv.at[2])
    keys = jnp.concatenate([got_kv[i, HD : 2 * HD] for i in range(seq_total)], axis=0)
    values_t = with_ones(
        jnp.concatenate([got_kv[i, 0:HD] for i in range(seq_total)], axis=1)
    )
    place = lax.div(seq, heads) * (4 * heads) + head * heads + lax.rem(seq, heads)
    units, unless_own = [], []
    for slots in BLOCKS:

        def upper_scores(slots=slots):
            for slot in slots:
                block = got_q.at[slot]
                pltpu.make_async_copy(block, block, recv_q.at[slot]).wait()
            block = jnp.concatenate([got_q[slot] for slot in slots], axis=1)
            return [dot_f32(keys, select_half(block, which)) for which in range(2)]

        def upper_masses(scores):
            row_max = jnp.maximum(
                *[jnp.max(part_scores, axis=0, keepdims=True) for part_scores in scores]
            )
            masses = [
                jnp.exp(part_scores - row_max).astype(jnp.bfloat16) for part_scores in scores
            ]
            pieces = []
            for i in range(seq_total):
                for which in range(2):
                    pieces.append(masses[which][i * HD : (i + 1) * HD])
            return row_max, jnp.concatenate(pieces, axis=0)

        def upper_sums(row_max, mass, slots=slots):
            weighted, logs = weigh(values_t, row_max, mass)
            for slot, begin in zip(slots, range(0, len(slots) * taken, taken)):
                for i in range(4):
                    lanes = slice(begin + i * part, begin + (i + 1) * part)
                    result[slot, i] = jnp.concatenate(
                        [weighted[16 * c : 16 * (c + 1), lanes] for c in range(4)], axis=1
                    )
                result_stat[slot] = logs[:, begin : begin + taken]
                for step in range(4):
                    i = lax.rem(head + step, 4)
                    pair_of_copies = [
                        pltpu.make_async_remote_copy(
                            src_ref=source,
                            dst_ref=target.at[place],
                            send_sem=sems.at[slot, step],
                            recv_sem=recv_sem,
                            device_id=(slot, i),
                            device_id_type=MESH,
                        )
                        for source, target, sems, recv_sem in (
                            (result.at[slot, i], returned, send_back, recv_back),
                            (result_stat.at[slot], returned_stat, send_stat, recv_stat),
                        )
                    ]
                    for copy in pair_of_copies:
                        if step:
                            copy.start()
                            waits.append(copy)
                        else:
                            pl.when(slot != seq)(copy.start)
                            unless_own.append((slot, copy))

                @pl.when(slot == seq)
                def _():
                    returned[place] = result[slot, head]
                    returned_stat[place] = result_stat[slot]

        units.append((upper_scores, upper_sums, upper_masses))
    pipelined(units, *UPPER_DEPTH)

    weight_arrived(across_head, common, 1)
    send_weight_rows(across_head, common, 5, (seq, beside_head))
    weight_arrived(across_head, others, 2)
    send_weight_rows(across_head, others, 6, (seq, beside_head))

    repeat = (
        (
            lax.broadcasted_iota(jnp.int32, (taken, rows), 0)
            == part * (lax.broadcasted_iota(jnp.int32, (taken, rows), 1) // taken)
            + (lax.broadcasted_iota(jnp.int32, (taken, rows), 1) % taken) // MIDDLE_DILATION
        )
        .astype(jnp.float32)
        .astype(jnp.bfloat16)
    )
    repeat_stat = (
        (
            lax.broadcasted_iota(jnp.int32, (taken, taken), 0)
            == part * head + lax.broadcasted_iota(jnp.int32, (taken, taken), 1) // MIDDLE_DILATION
        )
        .astype(jnp.float32)
        .astype(jnp.bfloat16)
    )
    arrived(bottom_got, 3, recv_bottom.at[0])
    arrived(bottom_stat_got, 3, recv_bottom.at[1])
    pairs = returned.shape[0]
    arrived(returned_stat, pairs - 1, recv_stat)
    logs = sum(
        dot_f32(value.astype(jnp.bfloat16), repeat_stat)
        for value in three_parts(returned_stat[...].reshape(pairs, taken))
    )

    def stat_rows(begin):
        return jnp.concatenate(
            [bottom_stat_got[i, begin : begin + heads] for i in range(4)], axis=0
        )

    all_logs = [stat_rows(0)]
    for level in range(2):
        level_logs = logs[level * 4 * heads : (level + 1) * 4 * heads]
        all_logs.append(level_logs + stat_rows((level + 1) * heads))
    highest = jnp.maximum(jnp.maximum(all_logs[0], all_logs[1]), all_logs[2])
    factors = [jnp.exp(one_log - highest) for one_log in all_logs]
    inverse = 1.0 / (factors[0] + factors[1] + factors[2])
    factors = [factor * inverse for factor in factors]

    arrived(returned, pairs - 1, recv_back)
    spread = dot_f32(returned[...].reshape(pairs * 16, taken), repeat)
    for one in range(4 * heads):
        for c in range(4):
            lanes = slice(c * taken, (c + 1) * taken)
            begin = (one % heads) * HD + 16 * c
            total = factors[0][one : one + 1] * bottom_got[
                one // heads, begin : begin + 16
            ].astype(jnp.float32)
            for level in range(2):
                at = (level * 4 * heads + one) * 16
                total += factors[level + 1][one : one + 1] * spread[at : at + 16, lanes]
            attention[one * HD + 16 * c : one * HD + 16 * (c + 1)] = total.astype(
                jnp.bfloat16
            )

    weight_arrived(beside_head, pl.ds(0, own_rows), 3)
    diagonal = 2 * (1 - chip) + (1 - core)
    weight_arrived(diagonal, mine, 4)
    weight_arrived(diagonal, common, 5)
    weight_arrived(diagonal, others, 6)
    projected = dot_f32(attention[0:own_rows].T, weights[0])
    for i in range(1, 4):
        projected += dot_f32(attention[i * own_rows : (i + 1) * own_rows].T, weights[i])
    out_ref[...] = projected.astype(out_ref.dtype)
    for copy in waits:
        copy.wait_send()
    for slot in range(1, seq_total):
        pltpu.make_async_copy(sent_q.at[0], sent_q.at[0], send_q.at[slot]).wait()
    for slot, copy in unless_own:
        pl.when(slot != seq)(copy.wait_send)


UPPER_DEPTH = (0, 0)
GATED_HALVES = 1
KV_ORDER = (4, 5, 6, 7, 1, 2, 3)
BLOCKS = ((0, 1), (2, 3), (4, 5), (6, 7))


def per_device_fused(query, key, value, middle_offsets, upper_offsets, out_weight):
    rows, width = query.shape
    seq_total = lax.axis_size("seq")
    heads = width // HD
    pairs = 2 * heads
    taken = rows // MIDDLE_DILATION
    anywhere = pl.BlockSpec(memory_space=pl.ANY)
    dma = pltpu.SemaphoreType.DMA
    bf16, f32 = jnp.bfloat16, jnp.float32
    return pl.pallas_call(
        functools.partial(fused_kernel, seq_total),
        out_shape=pltpu.VMEM((rows // 4, out_weight.shape[1]), bf16),
        in_specs=[anywhere] * 6,
        out_specs=pl.BlockSpec(memory_space=pltpu.VMEM),
        scratch_shapes=[
            pltpu.VMEM(query.shape, query.dtype),
            pltpu.VMEM(key.shape, key.dtype),
            pltpu.VMEM(value.shape, value.dtype),
            pltpu.SMEM(middle_offsets.shape, jnp.int32),
            pltpu.SMEM(upper_offsets.shape, jnp.int32),
            dma((6,)),
            pltpu.VMEM((pairs, 2 * HD, taken), bf16),
            pltpu.VMEM((pairs, HD, taken), bf16),
            pltpu.VMEM((seq_total, 2 * HD, taken), bf16),
            pltpu.VMEM((seq_total, HD, taken), bf16),
            pltpu.VMEM((seq_total, 4, 16, taken), bf16),
            pltpu.VMEM((seq_total, 1, taken), f32),
            pltpu.VMEM((4 * pairs, 16, taken), bf16),
            pltpu.VMEM((4 * pairs, 1, taken), f32),
            pltpu.VMEM((4, width, taken), bf16),
            pltpu.VMEM((4, 4 * heads, taken), f32),
            pltpu.VMEM((4, width, taken), bf16),
            pltpu.VMEM((4, 4 * heads, taken), f32),
            pltpu.VMEM((4,) + out_weight.shape, bf16),
            pltpu.VMEM((4 * width, taken), bf16),
            dma((seq_total,)),
            dma((3,)),
            dma((seq_total,)),
            dma((seq_total,)),
            dma((seq_total, 4)),
            dma,
            dma((seq_total, 4)),
            dma,
            dma((8,)),
            dma((2,)),
            dma((7,)),
            dma((7,)),
        ],
        compiler_params=pltpu.CompilerParams(
            collective_id=0, has_side_effects=True, vmem_limit_bytes=56 * 2**20
        ),
    )(query, key, value, middle_offsets, upper_offsets, out_weight)


def solution(mesh):
    in_specs = (
        P("seq", "head"),
        P("seq", "head"),
        P("seq", "head"),
        P("head"),
        P("head"),
        P("head", None),
    )
    out_specs = P(("seq", "head"), None)
    seq_total, head_shards = mesh.shape["seq"], mesh.shape["head"]
    one_segment = seq_total == SPAN and seq_total // 2 == MIDDLE_DILATION and head_shards == 4
    return jax.shard_map(
        per_device_fused if one_segment else per_device, mesh=mesh, in_specs=in_specs, out_specs=out_specs, check_vma=False
    )
```

```python
import functools

import jax
import jax.numpy as jnp
from jax import lax
from jax.experimental import pallas as pl
from jax.experimental.pallas import tpu as pltpu
from jax.sharding import PartitionSpec as P

HD = 64
SPAN = 8
MIDDLE_DILATION = 4


def partner_2(value, axis, stride):
    mask = 2**stride
    pairs = [(source, source ^ mask) for source in range(lax.axis_size(axis))]
    return lax.ppermute(value, axis, pairs)


def attend_segment(query_matrix_rows, key_matrix_rows, value_matrix_rows):
    scores = jnp.einsum(
        "qhd,khd->hqk", query_matrix_rows, key_matrix_rows, preferred_element_type=jnp.float32
    ) * HD ** (-0.5)
    row_max = jnp.max(scores, axis=2)
    mass = jnp.exp(scores - row_max[:, :, None])
    total = jnp.sum(mass, axis=2)
    soft_weights = mass.astype(jnp.bfloat16)
    weighted = jnp.einsum(
        "hqk,khd->qhd", soft_weights, value_matrix_rows, preferred_element_type=jnp.float32
    )
    return (weighted, total.T, row_max.T)


def attend_blocks(query_matrix_rows, key_matrix_rows, value_matrix_rows):
    block_size = min(512, query_matrix_rows.shape[0])
    pieces = query_matrix_rows.reshape(
        query_matrix_rows.shape[0] // block_size,
        block_size,
        query_matrix_rows.shape[1],
        query_matrix_rows.shape[2],
    )

    def one_block(one_piece):
        return attend_segment(one_piece, key_matrix_rows, value_matrix_rows)

    weighted, total, row_max = lax.map(one_block, pieces)
    return (
        weighted.reshape(query_matrix_rows.shape),
        total.reshape(query_matrix_rows.shape[:2]),
        row_max.reshape(query_matrix_rows.shape[:2]),
    )


def picked_rows(block_rows, offsets, stride):
    group_count = block_rows.shape[0] // stride
    grouped = block_rows.reshape(group_count, stride, block_rows.shape[1], block_rows.shape[2])
    chosen = (
        jnp.arange(stride, dtype=jnp.int32)[None, :, None, None] == offsets[None, None, :, None]
    )
    return jnp.sum(jnp.where(chosen, grouped, jnp.zeros((), grouped.dtype)), axis=1)


def scatter_rows(values, offsets, stride, filler):
    chosen = jnp.arange(stride, dtype=jnp.int32)[:, None] == offsets[None, :]
    spread_out = jnp.where(chosen[None], values[:, None], filler)
    return spread_out.reshape((values.shape[0] * stride,) + values.shape[1:])


def flatten_level(result):
    row_total = result[0].shape[0]
    weighted = result[0].reshape(row_total, -1)
    total = jnp.repeat(result[1], HD, axis=1)
    row_max = jnp.repeat(result[2], HD, axis=1)
    return (weighted, total, row_max)


def scatter_level(result, offsets, stride):
    weighted, total, row_max = flatten_level(result)
    column_offsets = jnp.repeat(offsets, HD)
    return (
        scatter_rows(weighted, column_offsets, stride, 0.0),
        scatter_rows(total, column_offsets, stride, 0.0),
        scatter_rows(row_max, column_offsets, stride, -jnp.inf),
    )


def combine(levels):
    highest = levels[0][2]
    for one_level in levels[1:]:
        highest = jnp.maximum(highest, one_level[2])
    numerator = jnp.zeros(levels[0][0].shape, jnp.float32)
    denominator = jnp.zeros(levels[0][1].shape, jnp.float32)
    for one_level in levels:
        factor = jnp.exp(one_level[2] - highest)
        numerator = numerator + factor * one_level[0]
        denominator = denominator + factor * one_level[1]
    return (numerator / denominator).astype(jnp.bfloat16)


def per_device(query, key, value, middle_offsets, upper_offsets, out_weight):
    row_count = query.shape[0]
    head_count = query.shape[1] // HD
    top_stride = lax.axis_size("seq") // 2
    query_matrix_rows = query.reshape(row_count, head_count, HD)
    key_matrix_rows = key.reshape(row_count, head_count, HD)
    value_matrix_rows = value.reshape(row_count, head_count, HD)
    top_key_local = picked_rows(key_matrix_rows, upper_offsets, top_stride).reshape(
        -1, head_count * HD
    )
    top_value_local = picked_rows(value_matrix_rows, upper_offsets, top_stride).reshape(
        -1, head_count * HD
    )
    top_key_all, top_value_all = (
        lax.all_gather(top_key_local, "seq", axis=0, tiled=True),
        lax.all_gather(top_value_local, "seq", axis=0, tiled=True),
    )
    upper_level = attend_segment(
        picked_rows(query_matrix_rows, upper_offsets, top_stride),
        top_key_all.reshape(-1, head_count, HD),
        top_value_all.reshape(-1, head_count, HD),
    )
    middle_pair = jnp.stack(
        [
            picked_rows(key_matrix_rows, middle_offsets, MIDDLE_DILATION),
            picked_rows(value_matrix_rows, middle_offsets, MIDDLE_DILATION),
        ]
    ).reshape(2, -1, head_count * HD)
    for bit_number in range(SPAN.bit_length() - 1):
        partner = partner_2(middle_pair, "seq", bit_number)
        middle_pair = jnp.concatenate([middle_pair, partner], axis=1)
    middle_level = attend_segment(
        picked_rows(query_matrix_rows, middle_offsets, MIDDLE_DILATION),
        middle_pair[0].reshape(-1, head_count, HD),
        middle_pair[1].reshape(-1, head_count, HD),
    )
    bottom = flatten_level(attend_blocks(query_matrix_rows, key_matrix_rows, value_matrix_rows))
    attention = combine(
        (
            bottom,
            scatter_level(middle_level, middle_offsets, MIDDLE_DILATION),
            scatter_level(upper_level, upper_offsets, top_stride),
        )
    )
    summed = lax.psum_scatter(
        jnp.dot(attention, out_weight, preferred_element_type=jnp.float32),
        "head",
        scatter_dimension=0,
        tiled=True,
    )
    return summed.astype(jnp.bfloat16)


MESH = pl.DeviceIdType.MESH
SHARED_ROWS = 96


def dot_f32(left, right):
    return jnp.dot(left, right, preferred_element_type=jnp.float32)


def three_parts(value):
    high = value.astype(jnp.bfloat16).astype(jnp.float32)
    rest = value - high
    middle = rest.astype(jnp.bfloat16).astype(jnp.float32)
    return [high, middle, rest - middle]


def softmax_of(scores):
    row_max = jnp.max(scores, axis=0, keepdims=True)
    return row_max, jnp.exp(scores - row_max).astype(jnp.bfloat16)


def weigh(values_with_ones, row_max, mass):
    summed = dot_f32(values_with_ones, mass)
    total = summed[HD : HD + 1]
    weighted = (summed[:HD] * (1.0 / total)).astype(jnp.bfloat16)
    return weighted, row_max + jnp.log(total)


def with_ones(values_t):
    ones = jnp.ones((16, values_t.shape[1]), values_t.dtype)
    return jnp.concatenate([values_t, ones], axis=0)


def pipelined(units, ahead, lag):
    scores, masses = {}, {}
    for i in range(len(units) + ahead + lag):
        if i < len(units):
            scores[i] = units[i][0]()
        j = i - ahead
        if 0 <= j < len(units):
            soften = units[j][2] if len(units[j]) > 2 else softmax_of
            masses[j] = soften(scores.pop(j))
        k = j - lag
        if 0 <= k < len(units):
            units[k][1](*masses.pop(k))


def select_half(block, which):
    blank = jnp.zeros_like(block)
    return jnp.concatenate([blank, block] if which else [block, blank], axis=0)


def fused_kernel(
    seq_total,
    query_hbm,
    key_hbm,
    value_hbm,
    middle_hbm,
    upper_hbm,
    weight_hbm,
    out_ref,
    query_ref,
    key_ref,
    value_ref,
    middle_ref,
    upper_ref,
    load,
    query_t,
    select,
    sent_kv,
    sent_q,
    got_kv,
    got_q,
    result,
    result_stat,
    returned,
    returned_stat,
    bottom,
    bottom_stat,
    bottom_got,
    bottom_stat_got,
    weights,
    attention,
    send_kv,
    recv_kv,
    send_q,
    recv_q,
    send_back,
    recv_back,
    send_stat,
    recv_stat,
    send_bottom,
    recv_bottom,
    send_weight,
    recv_weight,
):
    seq, head = lax.axis_index("seq"), lax.axis_index("head")
    chip, core = lax.div(head, 2), lax.rem(head, 2)
    beside_head = 2 * chip + (1 - core)
    across_head = 2 * (1 - chip) + core
    y = lax.rem(seq, 2)
    y_peer = seq + 1 - 2 * y
    rows = query_ref.shape[0]
    heads = query_ref.shape[1] // HD
    taken = rows // MIDDLE_DILATION
    part = taken // 4
    half_total = seq_total // 2
    offset_refs = (middle_ref, upper_ref)
    my_half, my_low = lax.div(seq, half_total), lax.rem(seq, half_total)
    my_inner = lax.rem(lax.div(seq, 2) + my_half, 2)

    def target_of(slot):
        half = lax.rem(my_half + slot // half_total, 2)
        return half * half_total + lax.rem(my_low + slot % half_total, half_total)

    z = lax.div(seq, 2)
    my_inner = lax.rem(z + my_half, 2)

    barrier = pltpu.get_barrier_semaphore()
    for step in range(1, seq_total):
        pl.semaphore_signal(
            barrier,
            inc=1,
            device_id=(lax.rem(seq + step, seq_total), head),
            device_id_type=MESH,
        )
    for step in range(1, 4):
        pl.semaphore_signal(
            barrier, inc=1, device_id=(seq, lax.rem(head + step, 4)), device_id_type=MESH
        )

    loads = []
    for i, (source, target) in enumerate(
        (
            (middle_hbm, middle_ref),
            (upper_hbm, upper_ref),
            (key_hbm, key_ref),
            (value_hbm, value_ref),
            (query_hbm, query_ref),
            (weight_hbm, weights.at[head]),
        )
    ):
        loads.append(pltpu.make_async_copy(source, target, load.at[i]))
    for copy in loads[:5]:
        copy.start()
    distance = lax.broadcasted_iota(jnp.int32, (taken, rows), 1) - MIDDLE_DILATION * (
        lax.broadcasted_iota(jnp.int32, (taken, rows), 0)
    )

    def pick(source_t, one, chosen):
        return lax.dot_general(
            source_t[one * HD : (one + 1) * HD],
            chosen,
            (((1,), (1,)), ((), ())),
            preferred_element_type=jnp.float32,
        ).astype(jnp.bfloat16)

    for copy in loads[:4]:
        copy.wait()
    value_t = value_ref[...].T
    for one in range(heads):
        for level in range(2):
            pair = level * heads + one
            chosen = jnp.where(
                distance == offset_refs[level][one], jnp.float32(1), jnp.float32(0)
            ).astype(jnp.bfloat16)
            select[pair] = chosen
            sent_kv[pair, 0:HD] = pick(value_t, one, chosen)
            picked = dot_f32(chosen, key_ref[:, one * HD : (one + 1) * HD])
            sent_kv[pair, HD : 2 * HD] = jnp.concatenate(
                [picked[: taken // 2], picked[taken // 2 :]], axis=1
            ).astype(jnp.bfloat16)

    def prepare_q():
        query_t[...] = (query_ref[...] * jnp.bfloat16(HD**-0.5)).T
        for one in range(heads):
            for level in range(2):
                pair = level * heads + one
                sent_q[pair] = pick(query_t, one, select[pair])

    loads[4].wait()
    pl.when(seq < EARLY_SHARDS)(prepare_q)
    pl.semaphore_wait(barrier, seq_total + 2)
    waits = []

    def send(source, target, send_sem, recv_sem, device):
        copy = pltpu.make_async_remote_copy(
            src_ref=source,
            dst_ref=target,
            send_sem=send_sem,
            recv_sem=recv_sem,
            device_id=device,
            device_id_type=MESH,
        )
        copy.start()
        return copy

    def send_kv_to(slot):
        to = target_of(slot)
        sem = recv_kv.at[my_inner] if slot >= half_total else recv_kv.at[2]
        waits.append(
            send(sent_kv.at[to], got_kv.at[seq], send_kv.at[slot], sem, (to, head))
        )

    def send_q_to(slot):
        to = target_of(slot)
        copy = pltpu.make_async_remote_copy(
            src_ref=sent_q.at[to],
            dst_ref=got_q.at[seq],
            send_sem=send_q.at[slot],
            recv_sem=recv_q.at[seq],
            device_id=(to, head),
            device_id_type=MESH,
        )
        copy.start()

    def send_far_q():
        for slot in range(half_total, seq_total):
            send_q_to(slot)

    pl.when(seq < EARLY_SHARDS)(send_far_q)
    for slot in KV_ORDER:
        send_kv_to(slot)
    loads[5].start()
    pl.when(seq >= EARLY_SHARDS)(prepare_q)
    got_kv[seq] = sent_kv[seq]
    own_q = pltpu.make_async_copy(sent_q.at[seq], got_q.at[seq], recv_q.at[seq])
    own_q.start()
    for slot in range(1, half_total):
        send_q_to(slot)
    in_between = jnp.logical_and(seq >= EARLY_SHARDS, seq < LATE_SHARDS)
    pl.when(in_between)(send_far_q)

    loads[5].wait()
    own_rows = weights.shape[1]
    middle_rows = own_rows - 2 * SHARED_ROWS
    mine = pl.ds(y * (own_rows - SHARED_ROWS), SHARED_ROWS)
    others = pl.ds((1 - y) * (own_rows - SHARED_ROWS), SHARED_ROWS)
    common = pl.ds(SHARED_ROWS, middle_rows)

    def send_weight_rows(which, part_rows, index, device):
        block = weights.at[which, part_rows]
        copy = send(block, block, send_weight.at[index], recv_weight.at[index], device)
        waits.append(copy)
        return copy

    def weight_arrived(which, part_rows, index):
        block = weights.at[which, part_rows]
        pltpu.make_async_copy(block, block, recv_weight.at[index]).wait()

    send_weight_rows(head, mine, 0, (seq, across_head))
    send_weight_rows(head, common, 1, (seq, across_head))
    send_weight_rows(head, pl.ds(0, own_rows), 3, (seq, beside_head))

    residue = lax.rem(lax.broadcasted_iota(jnp.int32, (1, taken), 1), MIDDLE_DILATION)
    half = rows // 2
    blocks = half // taken
    units = []
    for one in range(heads):
        for piece in range(2):

            def bottom_scores(one=one, piece=piece):
                both = slice(one // 2 * 2 * HD, (one // 2 + 1) * 2 * HD)
                block = query_t[one * HD : (one + 1) * HD, piece * half : (piece + 1) * half]
                return dot_f32(key_ref[:, both], select_half(block, one % 2))

            def bottom_sums(row_max, mass, one=one, piece=piece):
                span = slice(one * HD, (one + 1) * HD)
                weighted, logs = weigh(with_ones(value_t[span]), row_max, mass)
                for i in range(blocks):
                    cut = slice(i * taken, (i + 1) * taken)
                    bottom[piece * blocks + i, span] = weighted[:, cut]
                    bottom_stat[piece * blocks + i, one : one + 1] = logs[:, cut]

            units.append((bottom_scores, bottom_sums))
    pipelined(units, 2, 1)
    for one in range(heads):
        for level in range(2):
            bias = jnp.where(residue == offset_refs[level][one], 0.0, -jnp.inf)
            row = (level + 1) * heads + one
            for i in range(4):
                bottom_stat[i, row : row + 1] = bias
    for i in range(4):
        bottom_stat[i, 3 * heads :] = jnp.zeros((heads, taken), jnp.float32)

    for step in range(1, 4):
        to = lax.rem(head + step, 4)
        waits.append(
            send(
                bottom.at[to],
                bottom_got.at[head],
                send_bottom.at[step],
                recv_bottom.at[0],
                (seq, to),
            )
        )
        waits.append(
            send(
                bottom_stat.at[to],
                bottom_stat_got.at[head],
                send_bottom.at[4 + step],
                recv_bottom.at[1],
                (seq, to),
            )
        )
    bottom_got[head] = bottom[head]
    bottom_stat_got[head] = bottom_stat[head]

    def arrived(ref, count, sem):
        block = ref.at[pl.ds(0, count)]
        pltpu.make_async_copy(block, block, sem).wait()

    arrived(got_kv, 2, recv_kv.at[0])
    pl.when(seq >= LATE_SHARDS)(send_far_q)

    weight_arrived(across_head, mine, 0)
    send_weight_rows(across_head, mine, 2, (y_peer, head))
    send_weight_rows(across_head, mine, 4, (seq, beside_head))

    arrived(got_kv, 2, recv_kv.at[1])
    arrived(got_kv, half_total - 1, recv_kv.at[2])
    keys = jnp.concatenate([got_kv[i, HD : 2 * HD] for i in range(seq_total)], axis=0)
    values_t = with_ones(
        jnp.concatenate([got_kv[i, 0:HD] for i in range(seq_total)], axis=1)
    )
    place = lax.div(seq, heads) * (4 * heads) + head * heads + lax.rem(seq, heads)
    units, unless_own = [], []
    for slots in BLOCKS:

        def upper_scores(slots=slots):
            for slot in slots:
                block = got_q.at[slot]
                pltpu.make_async_copy(block, block, recv_q.at[slot]).wait()
            block = jnp.concatenate([got_q[slot] for slot in slots], axis=1)
            return [dot_f32(keys, select_half(block, which)) for which in range(2)]

        def upper_masses(scores):
            row_max = jnp.maximum(
                *[jnp.max(part_scores, axis=0, keepdims=True) for part_scores in scores]
            )
            masses = [
                jnp.exp(part_scores - row_max).astype(jnp.bfloat16) for part_scores in scores
            ]
            pieces = []
            for i in range(seq_total):
                for which in range(2):
                    pieces.append(masses[which][i * HD : (i + 1) * HD])
            return row_max, jnp.concatenate(pieces, axis=0)

        def upper_sums(row_max, mass, slots=slots):
            weighted, logs = weigh(values_t, row_max, mass)
            for slot, begin in zip(slots, range(0, len(slots) * taken, taken)):
                for i in range(4):
                    lanes = slice(begin + i * part, begin + (i + 1) * part)
                    result[slot, i] = jnp.concatenate(
                        [weighted[16 * c : 16 * (c + 1), lanes] for c in range(4)], axis=1
                    )
                result_stat[slot] = logs[:, begin : begin + taken]
                for step in range(4):
                    i = lax.rem(head + step, 4)
                    pair_of_copies = [
                        pltpu.make_async_remote_copy(
                            src_ref=source,
                            dst_ref=target.at[place],
                            send_sem=sems.at[slot, step],
                            recv_sem=recv_sem,
                            device_id=(slot, i),
                            device_id_type=MESH,
                        )
                        for source, target, sems, recv_sem in (
                            (result.at[slot, i], returned, send_back, recv_back),
                            (result_stat.at[slot], returned_stat, send_stat, recv_stat),
                        )
                    ]
                    for copy in pair_of_copies:
                        if step:
                            copy.start()
                            waits.append(copy)
                        else:
                            pl.when(slot != seq)(copy.start)
                            unless_own.append((slot, copy))

                @pl.when(slot == seq)
                def _():
                    returned[place] = result[slot, head]
                    returned_stat[place] = result_stat[slot]

        units.append((upper_scores, upper_sums, upper_masses))
    pipelined(units, *UPPER_DEPTH)

    weight_arrived(across_head, common, 1)
    send_weight_rows(across_head, common, 5, (seq, beside_head))
    weight_arrived(across_head, others, 2)
    send_weight_rows(across_head, others, 6, (seq, beside_head))

    repeat = (
        (
            lax.broadcasted_iota(jnp.int32, (taken, rows), 0)
            == part * (lax.broadcasted_iota(jnp.int32, (taken, rows), 1) // taken)
            + (lax.broadcasted_iota(jnp.int32, (taken, rows), 1) % taken) // MIDDLE_DILATION
        )
        .astype(jnp.float32)
        .astype(jnp.bfloat16)
    )
    repeat_stat = (
        (
            lax.broadcasted_iota(jnp.int32, (taken, taken), 0)
            == part * head + lax.broadcasted_iota(jnp.int32, (taken, taken), 1) // MIDDLE_DILATION
        )
        .astype(jnp.float32)
        .astype(jnp.bfloat16)
    )
    arrived(bottom_got, 3, recv_bottom.at[0])
    arrived(bottom_stat_got, 3, recv_bottom.at[1])
    pairs = returned.shape[0]
    arrived(returned_stat, pairs - 1, recv_stat)
    logs = sum(
        dot_f32(value.astype(jnp.bfloat16), repeat_stat)
        for value in three_parts(returned_stat[...].reshape(pairs, taken))
    )

    def stat_rows(begin):
        return jnp.concatenate(
            [bottom_stat_got[i, begin : begin + heads] for i in range(4)], axis=0
        )

    all_logs = [stat_rows(0)]
    for level in range(2):
        level_logs = logs[level * 4 * heads : (level + 1) * 4 * heads]
        all_logs.append(level_logs + stat_rows((level + 1) * heads))
    highest = jnp.maximum(jnp.maximum(all_logs[0], all_logs[1]), all_logs[2])
    factors = [jnp.exp(one_log - highest) for one_log in all_logs]
    inverse = 1.0 / (factors[0] + factors[1] + factors[2])
    factors = [factor * inverse for factor in factors]

    weight_arrived(beside_head, pl.ds(0, own_rows), 3)
    diagonal = 2 * (1 - chip) + (1 - core)
    weight_arrived(diagonal, mine, 4)
    weight_arrived(diagonal, common, 5)
    weight_arrived(diagonal, others, 6)
    arrived(returned, pairs - 1, recv_back)
    spread = dot_f32(returned[...].reshape(pairs * 16, taken), repeat)
    for one in range(4 * heads):
        for c in range(4):
            lanes = slice(c * taken, (c + 1) * taken)
            begin = (one % heads) * HD + 16 * c
            total = factors[0][one : one + 1] * bottom_got[
                one // heads, begin : begin + 16
            ].astype(jnp.float32)
            for level in range(2):
                at = (level * 4 * heads + one) * 16
                total += factors[level + 1][one : one + 1] * spread[at : at + 16, lanes]
            attention[one * HD + 16 * c : one * HD + 16 * (c + 1)] = total.astype(
                jnp.bfloat16
            )

    projected = dot_f32(attention[0:own_rows].T, weights[0])
    for i in range(1, 4):
        projected += dot_f32(attention[i * own_rows : (i + 1) * own_rows].T, weights[i])
    out_ref[...] = projected.astype(out_ref.dtype)
    for copy in waits:
        copy.wait_send()
    for slot in range(1, seq_total):
        pltpu.make_async_copy(sent_q.at[0], sent_q.at[0], send_q.at[slot]).wait()
    for slot, copy in unless_own:
        pl.when(slot != seq)(copy.wait_send)


UPPER_DEPTH = (0, 0)
EARLY_SHARDS, LATE_SHARDS = 2, 8
KV_ORDER = (4, 5, 6, 7, 1, 2, 3)
BLOCKS = ((0,), (1,), (2, 3), (4, 5), (6, 7))


def per_device_fused(query, key, value, middle_offsets, upper_offsets, out_weight):
    rows, width = query.shape
    seq_total = lax.axis_size("seq")
    heads = width // HD
    pairs = 2 * heads
    taken = rows // MIDDLE_DILATION
    anywhere = pl.BlockSpec(memory_space=pl.ANY)
    dma = pltpu.SemaphoreType.DMA
    bf16, f32 = jnp.bfloat16, jnp.float32
    return pl.pallas_call(
        functools.partial(fused_kernel, seq_total),
        out_shape=pltpu.VMEM((rows // 4, out_weight.shape[1]), bf16),
        in_specs=[anywhere] * 6,
        out_specs=pl.BlockSpec(memory_space=pltpu.VMEM),
        scratch_shapes=[
            pltpu.VMEM(query.shape, query.dtype),
            pltpu.VMEM(key.shape, key.dtype),
            pltpu.VMEM(value.shape, value.dtype),
            pltpu.SMEM(middle_offsets.shape, jnp.int32),
            pltpu.SMEM(upper_offsets.shape, jnp.int32),
            dma((6,)),
            pltpu.VMEM((width, rows), bf16),
            pltpu.VMEM((pairs, taken, rows), bf16),
            pltpu.VMEM((pairs, 2 * HD, taken), bf16),
            pltpu.VMEM((pairs, HD, taken), bf16),
            pltpu.VMEM((seq_total, 2 * HD, taken), bf16),
            pltpu.VMEM((seq_total, HD, taken), bf16),
            pltpu.VMEM((seq_total, 4, 16, taken), bf16),
            pltpu.VMEM((seq_total, 1, taken), f32),
            pltpu.VMEM((4 * pairs, 16, taken), bf16),
            pltpu.VMEM((4 * pairs, 1, taken), f32),
            pltpu.VMEM((4, width, taken), bf16),
            pltpu.VMEM((4, 4 * heads, taken), f32),
            pltpu.VMEM((4, width, taken), bf16),
            pltpu.VMEM((4, 4 * heads, taken), f32),
            pltpu.VMEM((4,) + out_weight.shape, bf16),
            pltpu.VMEM((4 * width, taken), bf16),
            dma((seq_total,)),
            dma((3,)),
            dma((seq_total,)),
            dma((seq_total,)),
            dma((seq_total, 4)),
            dma,
            dma((seq_total, 4)),
            dma,
            dma((8,)),
            dma((2,)),
            dma((7,)),
            dma((7,)),
        ],
        compiler_params=pltpu.CompilerParams(
            collective_id=0, has_side_effects=True, vmem_limit_bytes=56 * 2**20
        ),
    )(query, key, value, middle_offsets, upper_offsets, out_weight)


def solution(mesh):
    in_specs = (
        P("seq", "head"),
        P("seq", "head"),
        P("seq", "head"),
        P("head"),
        P("head"),
        P("head", None),
    )
    out_specs = P(("seq", "head"), None)
    seq_total, head_shards = mesh.shape["seq"], mesh.shape["head"]
    one_segment = seq_total == SPAN and seq_total // 2 == MIDDLE_DILATION and head_shards == 4
    return jax.shard_map(
        per_device_fused if one_segment else per_device, mesh=mesh, in_specs=in_specs, out_specs=out_specs, check_vma=False
    )
```

```python
import functools

import jax
import jax.numpy as jnp
from jax import lax
from jax.experimental import pallas as pl
from jax.experimental.pallas import tpu as pltpu
from jax.sharding import PartitionSpec as P

HD = 64
SPAN = 8
MIDDLE_DILATION = 4


def partner_2(value, axis, stride):
    mask = 2**stride
    pairs = [(source, source ^ mask) for source in range(lax.axis_size(axis))]
    return lax.ppermute(value, axis, pairs)


def attend_segment(query_matrix_rows, key_matrix_rows, value_matrix_rows):
    scores = jnp.einsum(
        "qhd,khd->hqk", query_matrix_rows, key_matrix_rows, preferred_element_type=jnp.float32
    ) * HD ** (-0.5)
    row_max = jnp.max(scores, axis=2)
    mass = jnp.exp(scores - row_max[:, :, None])
    total = jnp.sum(mass, axis=2)
    soft_weights = mass.astype(jnp.bfloat16)
    weighted = jnp.einsum(
        "hqk,khd->qhd", soft_weights, value_matrix_rows, preferred_element_type=jnp.float32
    )
    return (weighted, total.T, row_max.T)


def attend_blocks(query_matrix_rows, key_matrix_rows, value_matrix_rows):
    block_size = min(512, query_matrix_rows.shape[0])
    pieces = query_matrix_rows.reshape(
        query_matrix_rows.shape[0] // block_size,
        block_size,
        query_matrix_rows.shape[1],
        query_matrix_rows.shape[2],
    )

    def one_block(one_piece):
        return attend_segment(one_piece, key_matrix_rows, value_matrix_rows)

    weighted, total, row_max = lax.map(one_block, pieces)
    return (
        weighted.reshape(query_matrix_rows.shape),
        total.reshape(query_matrix_rows.shape[:2]),
        row_max.reshape(query_matrix_rows.shape[:2]),
    )


def picked_rows(block_rows, offsets, stride):
    group_count = block_rows.shape[0] // stride
    grouped = block_rows.reshape(group_count, stride, block_rows.shape[1], block_rows.shape[2])
    chosen = (
        jnp.arange(stride, dtype=jnp.int32)[None, :, None, None] == offsets[None, None, :, None]
    )
    return jnp.sum(jnp.where(chosen, grouped, jnp.zeros((), grouped.dtype)), axis=1)


def scatter_rows(values, offsets, stride, filler):
    chosen = jnp.arange(stride, dtype=jnp.int32)[:, None] == offsets[None, :]
    spread_out = jnp.where(chosen[None], values[:, None], filler)
    return spread_out.reshape((values.shape[0] * stride,) + values.shape[1:])


def flatten_level(result):
    row_total = result[0].shape[0]
    weighted = result[0].reshape(row_total, -1)
    total = jnp.repeat(result[1], HD, axis=1)
    row_max = jnp.repeat(result[2], HD, axis=1)
    return (weighted, total, row_max)


def scatter_level(result, offsets, stride):
    weighted, total, row_max = flatten_level(result)
    column_offsets = jnp.repeat(offsets, HD)
    return (
        scatter_rows(weighted, column_offsets, stride, 0.0),
        scatter_rows(total, column_offsets, stride, 0.0),
        scatter_rows(row_max, column_offsets, stride, -jnp.inf),
    )


def combine(levels):
    highest = levels[0][2]
    for one_level in levels[1:]:
        highest = jnp.maximum(highest, one_level[2])
    numerator = jnp.zeros(levels[0][0].shape, jnp.float32)
    denominator = jnp.zeros(levels[0][1].shape, jnp.float32)
    for one_level in levels:
        factor = jnp.exp(one_level[2] - highest)
        numerator = numerator + factor * one_level[0]
        denominator = denominator + factor * one_level[1]
    return (numerator / denominator).astype(jnp.bfloat16)


def per_device(query, key, value, middle_offsets, upper_offsets, out_weight):
    row_count = query.shape[0]
    head_count = query.shape[1] // HD
    top_stride = lax.axis_size("seq") // 2
    query_matrix_rows = query.reshape(row_count, head_count, HD)
    key_matrix_rows = key.reshape(row_count, head_count, HD)
    value_matrix_rows = value.reshape(row_count, head_count, HD)
    top_key_local = picked_rows(key_matrix_rows, upper_offsets, top_stride).reshape(
        -1, head_count * HD
    )
    top_value_local = picked_rows(value_matrix_rows, upper_offsets, top_stride).reshape(
        -1, head_count * HD
    )
    top_key_all, top_value_all = (
        lax.all_gather(top_key_local, "seq", axis=0, tiled=True),
        lax.all_gather(top_value_local, "seq", axis=0, tiled=True),
    )
    upper_level = attend_segment(
        picked_rows(query_matrix_rows, upper_offsets, top_stride),
        top_key_all.reshape(-1, head_count, HD),
        top_value_all.reshape(-1, head_count, HD),
    )
    middle_pair = jnp.stack(
        [
            picked_rows(key_matrix_rows, middle_offsets, MIDDLE_DILATION),
            picked_rows(value_matrix_rows, middle_offsets, MIDDLE_DILATION),
        ]
    ).reshape(2, -1, head_count * HD)
    for bit_number in range(SPAN.bit_length() - 1):
        partner = partner_2(middle_pair, "seq", bit_number)
        middle_pair = jnp.concatenate([middle_pair, partner], axis=1)
    middle_level = attend_segment(
        picked_rows(query_matrix_rows, middle_offsets, MIDDLE_DILATION),
        middle_pair[0].reshape(-1, head_count, HD),
        middle_pair[1].reshape(-1, head_count, HD),
    )
    bottom = flatten_level(attend_blocks(query_matrix_rows, key_matrix_rows, value_matrix_rows))
    attention = combine(
        (
            bottom,
            scatter_level(middle_level, middle_offsets, MIDDLE_DILATION),
            scatter_level(upper_level, upper_offsets, top_stride),
        )
    )
    summed = lax.psum_scatter(
        jnp.dot(attention, out_weight, preferred_element_type=jnp.float32),
        "head",
        scatter_dimension=0,
        tiled=True,
    )
    return summed.astype(jnp.bfloat16)


MESH = pl.DeviceIdType.MESH
SHARED_ROWS = 96


def dot_f32(left, right):
    return jnp.dot(left, right, preferred_element_type=jnp.float32)


def three_parts(value):
    high = value.astype(jnp.bfloat16).astype(jnp.float32)
    rest = value - high
    middle = rest.astype(jnp.bfloat16).astype(jnp.float32)
    return [high, middle, rest - middle]


def softmax_of(scores):
    row_max = jnp.max(scores, axis=0, keepdims=True)
    return row_max, jnp.exp(scores - row_max).astype(jnp.bfloat16)


def weigh(values_with_ones, row_max, mass):
    summed = dot_f32(values_with_ones, mass)
    total = summed[HD : HD + 1]
    weighted = (summed[:HD] * (1.0 / total)).astype(jnp.bfloat16)
    return weighted, row_max + jnp.log(total)


def with_ones(values_t):
    ones = jnp.ones((16, values_t.shape[1]), values_t.dtype)
    return jnp.concatenate([values_t, ones], axis=0)


def pipelined(units, ahead, lag):
    scores, masses = {}, {}
    for i in range(len(units) + ahead + lag):
        if i < len(units):
            scores[i] = units[i][0]()
        j = i - ahead
        if 0 <= j < len(units):
            soften = units[j][2] if len(units[j]) > 2 else softmax_of
            masses[j] = soften(scores.pop(j))
        k = j - lag
        if 0 <= k < len(units):
            units[k][1](*masses.pop(k))


def select_half(block, which):
    blank = jnp.zeros_like(block)
    return jnp.concatenate([blank, block] if which else [block, blank], axis=0)


def fused_kernel(
    seq_total,
    query_hbm,
    key_hbm,
    value_hbm,
    middle_hbm,
    upper_hbm,
    weight_hbm,
    out_ref,
    query_ref,
    key_ref,
    value_ref,
    middle_ref,
    upper_ref,
    load,
    query_t,
    select,
    sent_kv,
    sent_q,
    got_kv,
    got_q,
    result,
    result_stat,
    returned,
    returned_stat,
    bottom,
    bottom_stat,
    bottom_got,
    bottom_stat_got,
    weights,
    attention,
    send_kv,
    recv_kv,
    send_q,
    recv_q,
    send_back,
    recv_back,
    send_stat,
    recv_stat,
    send_bottom,
    recv_bottom,
    send_weight,
    recv_weight,
):
    seq, head = lax.axis_index("seq"), lax.axis_index("head")
    chip, core = lax.div(head, 2), lax.rem(head, 2)
    beside_head = 2 * chip + (1 - core)
    across_head = 2 * (1 - chip) + core
    y = lax.rem(seq, 2)
    y_peer = seq + 1 - 2 * y
    rows = query_ref.shape[0]
    heads = query_ref.shape[1] // HD
    taken = rows // MIDDLE_DILATION
    part = taken // 4
    half_total = seq_total // 2
    offset_refs = (middle_ref, upper_ref)
    my_half, my_low = lax.div(seq, half_total), lax.rem(seq, half_total)
    my_inner = lax.rem(lax.div(seq, 2) + my_half, 2)

    def target_of(slot):
        half = lax.rem(my_half + slot // half_total, 2)
        return half * half_total + lax.rem(my_low + slot % half_total, half_total)

    z = lax.div(seq, 2)
    my_inner = lax.rem(z + my_half, 2)

    loads = []
    for i, (source, target) in enumerate(
        (
            (value_hbm, value_ref),
            (key_hbm, key_ref),
            (middle_hbm, middle_ref),
            (upper_hbm, upper_ref),
            (query_hbm, query_ref),
            (weight_hbm, weights.at[head]),
        )
    ):
        loads.append(pltpu.make_async_copy(source, target, load.at[i]))
    for copy in loads[:4]:
        copy.start()

    barrier = pltpu.get_barrier_semaphore()
    for step in range(1, seq_total):
        pl.semaphore_signal(
            barrier,
            inc=1,
            device_id=(lax.rem(seq + step, seq_total), head),
            device_id_type=MESH,
        )
    for step in range(1, 4):
        pl.semaphore_signal(
            barrier, inc=1, device_id=(seq, lax.rem(head + step, 4)), device_id_type=MESH
        )

    loads[4].start()
    distance = lax.broadcasted_iota(jnp.int32, (taken, rows), 1) - MIDDLE_DILATION * (
        lax.broadcasted_iota(jnp.int32, (taken, rows), 0)
    )

    def pick(source_t, one, chosen):
        return lax.dot_general(
            source_t[one * HD : (one + 1) * HD],
            chosen,
            (((1,), (1,)), ((), ())),
            preferred_element_type=jnp.float32,
        ).astype(jnp.bfloat16)

    for copy in loads[:4]:
        copy.wait()
    loads[5].start()
    value_t = value_ref[...].T
    for one in range(heads):
        for level in range(2):
            pair = level * heads + one
            chosen = jnp.where(
                distance == offset_refs[level][one], jnp.float32(1), jnp.float32(0)
            ).astype(jnp.bfloat16)
            select[pair] = chosen
            sent_kv[pair, 0:HD] = pick(value_t, one, chosen)
            picked = dot_f32(chosen, key_ref[:, one * HD : (one + 1) * HD])
            sent_kv[pair, HD : 2 * HD] = jnp.concatenate(
                [picked[: taken // 2], picked[taken // 2 :]], axis=1
            ).astype(jnp.bfloat16)

    def prepare_q():
        query_t[...] = (query_ref[...] * jnp.bfloat16(HD**-0.5)).T
        for one in range(heads):
            for level in range(2):
                pair = level * heads + one
                sent_q[pair] = pick(query_t, one, select[pair])

    loads[4].wait()
    pl.when(seq < EARLY_SHARDS)(prepare_q)
    pl.semaphore_wait(barrier, seq_total + 2)
    waits = []

    def send(source, target, send_sem, recv_sem, device):
        copy = pltpu.make_async_remote_copy(
            src_ref=source,
            dst_ref=target,
            send_sem=send_sem,
            recv_sem=recv_sem,
            device_id=device,
            device_id_type=MESH,
        )
        copy.start()
        return copy

    def send_kv_to(slot):
        to = target_of(slot)
        sem = recv_kv.at[my_inner] if slot >= half_total else recv_kv.at[2]
        waits.append(
            send(sent_kv.at[to], got_kv.at[seq], send_kv.at[slot], sem, (to, head))
        )

    def send_q_to(slot):
        to = target_of(slot)
        copy = pltpu.make_async_remote_copy(
            src_ref=sent_q.at[to],
            dst_ref=got_q.at[seq],
            send_sem=send_q.at[slot],
            recv_sem=recv_q.at[seq],
            device_id=(to, head),
            device_id_type=MESH,
        )
        copy.start()

    def send_far_q():
        for slot in range(half_total, seq_total):
            send_q_to(slot)

    pl.when(seq < EARLY_SHARDS)(send_far_q)
    for slot in KV_ORDER:
        send_kv_to(slot)
    loads[5].wait()
    own_rows = weights.shape[1]
    middle_rows = own_rows - 2 * SHARED_ROWS
    mine = pl.ds(y * (own_rows - SHARED_ROWS), SHARED_ROWS)
    others = pl.ds((1 - y) * (own_rows - SHARED_ROWS), SHARED_ROWS)
    common = pl.ds(SHARED_ROWS, middle_rows)

    def send_weight_rows(which, part_rows, index, device):
        block = weights.at[which, part_rows]
        copy = send(block, block, send_weight.at[index], recv_weight.at[index], device)
        waits.append(copy)
        return copy

    def weight_arrived(which, part_rows, index):
        block = weights.at[which, part_rows]
        pltpu.make_async_copy(block, block, recv_weight.at[index]).wait()

    send_weight_rows(head, mine, 0, (seq, across_head))
    send_weight_rows(head, common, 1, (seq, across_head))
    send_weight_rows(head, pl.ds(0, own_rows), 3, (seq, beside_head))
    pl.when(seq >= EARLY_SHARDS)(prepare_q)
    got_kv[seq] = sent_kv[seq]
    own_q = pltpu.make_async_copy(sent_q.at[seq], got_q.at[seq], recv_q.at[seq])
    own_q.start()
    for slot in range(1, half_total):
        send_q_to(slot)
    in_between = jnp.logical_and(seq >= EARLY_SHARDS, seq < LATE_SHARDS)
    pl.when(in_between)(send_far_q)

    residue = lax.rem(lax.broadcasted_iota(jnp.int32, (1, taken), 1), MIDDLE_DILATION)
    half = rows // 2
    blocks = half // taken
    units = []
    for one in range(heads):
        for piece in range(2):

            def bottom_scores(one=one, piece=piece):
                both = slice(one // 2 * 2 * HD, (one // 2 + 1) * 2 * HD)
                block = query_t[one * HD : (one + 1) * HD, piece * half : (piece + 1) * half]
                return dot_f32(key_ref[:, both], select_half(block, one % 2))

            def bottom_sums(row_max, mass, one=one, piece=piece):
                span = slice(one * HD, (one + 1) * HD)
                weighted, logs = weigh(with_ones(value_t[span]), row_max, mass)
                for i in range(blocks):
                    cut = slice(i * taken, (i + 1) * taken)
                    bottom[piece * blocks + i, span] = weighted[:, cut]
                    bottom_stat[piece * blocks + i, one : one + 1] = logs[:, cut]

            units.append((bottom_scores, bottom_sums))
    pipelined(units, 2, 1)
    for one in range(heads):
        for level in range(2):
            bias = jnp.where(residue == offset_refs[level][one], 0.0, -jnp.inf)
            row = (level + 1) * heads + one
            for i in range(4):
                bottom_stat[i, row : row + 1] = bias
    for i in range(4):
        bottom_stat[i, 3 * heads :] = jnp.zeros((heads, taken), jnp.float32)

    for step in range(1, 4):
        to = lax.rem(head + step, 4)
        waits.append(
            send(
                bottom.at[to],
                bottom_got.at[head],
                send_bottom.at[step],
                recv_bottom.at[0],
                (seq, to),
            )
        )
        waits.append(
            send(
                bottom_stat.at[to],
                bottom_stat_got.at[head],
                send_bottom.at[4 + step],
                recv_bottom.at[1],
                (seq, to),
            )
        )
    bottom_got[head] = bottom[head]
    bottom_stat_got[head] = bottom_stat[head]

    def arrived(ref, count, sem):
        block = ref.at[pl.ds(0, count)]
        pltpu.make_async_copy(block, block, sem).wait()

    arrived(got_kv, 2, recv_kv.at[0])
    pl.when(seq >= LATE_SHARDS)(send_far_q)

    weight_arrived(across_head, mine, 0)
    send_weight_rows(across_head, mine, 2, (y_peer, head))
    send_weight_rows(across_head, mine, 4, (seq, beside_head))

    arrived(got_kv, 2, recv_kv.at[1])
    arrived(got_kv, half_total - 1, recv_kv.at[2])
    keys = jnp.concatenate([got_kv[i, HD : 2 * HD] for i in range(seq_total)], axis=0)
    values_t = with_ones(
        jnp.concatenate([got_kv[i, 0:HD] for i in range(seq_total)], axis=1)
    )
    place = lax.div(seq, heads) * (4 * heads) + head * heads + lax.rem(seq, heads)
    units, unless_own = [], []
    for slots in BLOCKS:

        def upper_scores(slots=slots):
            for slot in slots:
                block = got_q.at[slot]
                pltpu.make_async_copy(block, block, recv_q.at[slot]).wait()
            block = jnp.concatenate([got_q[slot] for slot in slots], axis=1)
            return [dot_f32(keys, select_half(block, which)) for which in range(2)]

        def upper_masses(scores):
            row_max = jnp.maximum(
                *[jnp.max(part_scores, axis=0, keepdims=True) for part_scores in scores]
            )
            masses = [
                jnp.exp(part_scores - row_max).astype(jnp.bfloat16) for part_scores in scores
            ]
            pieces = []
            for i in range(seq_total):
                for which in range(2):
                    pieces.append(masses[which][i * HD : (i + 1) * HD])
            return row_max, jnp.concatenate(pieces, axis=0)

        def upper_sums(row_max, mass, slots=slots):
            weighted, logs = weigh(values_t, row_max, mass)
            for slot, begin in zip(slots, range(0, len(slots) * taken, taken)):
                for i in range(4):
                    lanes = slice(begin + i * part, begin + (i + 1) * part)
                    result[slot, i] = jnp.concatenate(
                        [weighted[16 * c : 16 * (c + 1), lanes] for c in range(4)], axis=1
                    )
                result_stat[slot] = logs[:, begin : begin + taken]
                for step in range(4):
                    i = lax.rem(head + step, 4)
                    pair_of_copies = [
                        pltpu.make_async_remote_copy(
                            src_ref=source,
                            dst_ref=target.at[place],
                            send_sem=sems.at[slot, step],
                            recv_sem=recv_sem,
                            device_id=(slot, i),
                            device_id_type=MESH,
                        )
                        for source, target, sems, recv_sem in (
                            (result.at[slot, i], returned, send_back, recv_back),
                            (result_stat.at[slot], returned_stat, send_stat, recv_stat),
                        )
                    ]
                    for copy in pair_of_copies:
                        if step:
                            copy.start()
                            waits.append(copy)
                        else:
                            pl.when(slot != seq)(copy.start)
                            unless_own.append((slot, copy))

                @pl.when(slot == seq)
                def _():
                    returned[place] = result[slot, head]
                    returned_stat[place] = result_stat[slot]

        units.append((upper_scores, upper_sums, upper_masses))
    pipelined(units[:ALONE], 0, 0)
    pipelined(units[ALONE:], *UPPER_DEPTH)

    weight_arrived(across_head, common, 1)
    send_weight_rows(across_head, common, 5, (seq, beside_head))
    weight_arrived(across_head, others, 2)
    send_weight_rows(across_head, others, 6, (seq, beside_head))

    repeat = (
        (
            lax.broadcasted_iota(jnp.int32, (taken, rows), 0)
            == part * (lax.broadcasted_iota(jnp.int32, (taken, rows), 1) // taken)
            + (lax.broadcasted_iota(jnp.int32, (taken, rows), 1) % taken) // MIDDLE_DILATION
        )
        .astype(jnp.float32)
        .astype(jnp.bfloat16)
    )
    repeat_stat = (
        (
            lax.broadcasted_iota(jnp.int32, (taken, taken), 0)
            == part * head + lax.broadcasted_iota(jnp.int32, (taken, taken), 1) // MIDDLE_DILATION
        )
        .astype(jnp.float32)
        .astype(jnp.bfloat16)
    )
    arrived(bottom_got, 3, recv_bottom.at[0])
    arrived(bottom_stat_got, 3, recv_bottom.at[1])
    pairs = returned.shape[0]
    arrived(returned_stat, pairs - 1, recv_stat)
    logs = sum(
        dot_f32(value.astype(jnp.bfloat16), repeat_stat)
        for value in three_parts(returned_stat[...].reshape(pairs, taken))
    )

    def stat_rows(begin):
        return jnp.concatenate(
            [bottom_stat_got[i, begin : begin + heads] for i in range(4)], axis=0
        )

    all_logs = [stat_rows(0)]
    for level in range(2):
        level_logs = logs[level * 4 * heads : (level + 1) * 4 * heads]
        all_logs.append(level_logs + stat_rows((level + 1) * heads))
    highest = jnp.maximum(jnp.maximum(all_logs[0], all_logs[1]), all_logs[2])
    factors = [jnp.exp(one_log - highest) for one_log in all_logs]
    inverse = 1.0 / (factors[0] + factors[1] + factors[2])
    factors = [factor * inverse for factor in factors]

    weight_arrived(beside_head, pl.ds(0, own_rows), 3)
    diagonal = 2 * (1 - chip) + (1 - core)
    weight_arrived(diagonal, mine, 4)
    weight_arrived(diagonal, common, 5)
    weight_arrived(diagonal, others, 6)
    arrived(returned, pairs - 1, recv_back)
    spread = dot_f32(returned[...].reshape(pairs * 16, taken), repeat)
    for one in range(4 * heads):
        for c in range(4):
            lanes = slice(c * taken, (c + 1) * taken)
            begin = (one % heads) * HD + 16 * c
            total = factors[0][one : one + 1] * bottom_got[
                one // heads, begin : begin + 16
            ].astype(jnp.float32)
            for level in range(2):
                at = (level * 4 * heads + one) * 16
                total += factors[level + 1][one : one + 1] * spread[at : at + 16, lanes]
            attention[one * HD + 16 * c : one * HD + 16 * (c + 1)] = total.astype(
                jnp.bfloat16
            )

    projected = dot_f32(attention[0:own_rows].T, weights[0])
    for i in range(1, 4):
        projected += dot_f32(attention[i * own_rows : (i + 1) * own_rows].T, weights[i])
    out_ref[...] = projected.astype(out_ref.dtype)
    for copy in waits:
        copy.wait_send()
    for slot in range(1, seq_total):
        pltpu.make_async_copy(sent_q.at[0], sent_q.at[0], send_q.at[slot]).wait()
    for slot, copy in unless_own:
        pl.when(slot != seq)(copy.wait_send)


ALONE = 1
UPPER_DEPTH = (1, 0)
EARLY_SHARDS, LATE_SHARDS = 2, 8
KV_ORDER = (4, 5, 6, 7, 1, 2, 3)
BLOCKS = ((0,), (1,), (2, 3), (4, 5), (6, 7))


def per_device_fused(query, key, value, middle_offsets, upper_offsets, out_weight):
    rows, width = query.shape
    seq_total = lax.axis_size("seq")
    heads = width // HD
    pairs = 2 * heads
    taken = rows // MIDDLE_DILATION
    anywhere = pl.BlockSpec(memory_space=pl.ANY)
    dma = pltpu.SemaphoreType.DMA
    bf16, f32 = jnp.bfloat16, jnp.float32
    return pl.pallas_call(
        functools.partial(fused_kernel, seq_total),
        out_shape=pltpu.VMEM((rows // 4, out_weight.shape[1]), bf16),
        in_specs=[anywhere] * 6,
        out_specs=pl.BlockSpec(memory_space=pltpu.VMEM),
        scratch_shapes=[
            pltpu.VMEM(query.shape, query.dtype),
            pltpu.VMEM(key.shape, key.dtype),
            pltpu.VMEM(value.shape, value.dtype),
            pltpu.SMEM(middle_offsets.shape, jnp.int32),
            pltpu.SMEM(upper_offsets.shape, jnp.int32),
            dma((6,)),
            pltpu.VMEM((width, rows), bf16),
            pltpu.VMEM((pairs, taken, rows), bf16),
            pltpu.VMEM((pairs, 2 * HD, taken), bf16),
            pltpu.VMEM((pairs, HD, taken), bf16),
            pltpu.VMEM((seq_total, 2 * HD, taken), bf16),
            pltpu.VMEM((seq_total, HD, taken), bf16),
            pltpu.VMEM((seq_total, 4, 16, taken), bf16),
            pltpu.VMEM((seq_total, 1, taken), f32),
            pltpu.VMEM((4 * pairs, 16, taken), bf16),
            pltpu.VMEM((4 * pairs, 1, taken), f32),
            pltpu.VMEM((4, width, taken), bf16),
            pltpu.VMEM((4, 4 * heads, taken), f32),
            pltpu.VMEM((4, width, taken), bf16),
            pltpu.VMEM((4, 4 * heads, taken), f32),
            pltpu.VMEM((4,) + out_weight.shape, bf16),
            pltpu.VMEM((4 * width, taken), bf16),
            dma((seq_total,)),
            dma((3,)),
            dma((seq_total,)),
            dma((seq_total,)),
            dma((seq_total, 4)),
            dma,
            dma((seq_total, 4)),
            dma,
            dma((8,)),
            dma((2,)),
            dma((7,)),
            dma((7,)),
        ],
        compiler_params=pltpu.CompilerParams(
            collective_id=0, has_side_effects=True, vmem_limit_bytes=56 * 2**20
        ),
    )(query, key, value, middle_offsets, upper_offsets, out_weight)


def solution(mesh):
    in_specs = (
        P("seq", "head"),
        P("seq", "head"),
        P("seq", "head"),
        P("head"),
        P("head"),
        P("head", None),
    )
    out_specs = P(("seq", "head"), None)
    seq_total, head_shards = mesh.shape["seq"], mesh.shape["head"]
    one_segment = seq_total == SPAN and seq_total // 2 == MIDDLE_DILATION and head_shards == 4
    return jax.shard_map(
        per_device_fused if one_segment else per_device, mesh=mesh, in_specs=in_specs, out_specs=out_specs, check_vma=False
    )
```

```python
import functools

import jax
import jax.numpy as jnp
from jax import lax
from jax.experimental import pallas as pl
from jax.experimental.pallas import tpu as pltpu
from jax.sharding import PartitionSpec as P

HD = 64
SPAN = 8
MIDDLE_DILATION = 4


def partner_2(value, axis, stride):
    mask = 2**stride
    pairs = [(source, source ^ mask) for source in range(lax.axis_size(axis))]
    return lax.ppermute(value, axis, pairs)


def attend_segment(query_matrix_rows, key_matrix_rows, value_matrix_rows):
    scores = jnp.einsum(
        "qhd,khd->hqk", query_matrix_rows, key_matrix_rows, preferred_element_type=jnp.float32
    ) * HD ** (-0.5)
    row_max = jnp.max(scores, axis=2)
    mass = jnp.exp(scores - row_max[:, :, None])
    total = jnp.sum(mass, axis=2)
    soft_weights = mass.astype(jnp.bfloat16)
    weighted = jnp.einsum(
        "hqk,khd->qhd", soft_weights, value_matrix_rows, preferred_element_type=jnp.float32
    )
    return (weighted, total.T, row_max.T)


def attend_blocks(query_matrix_rows, key_matrix_rows, value_matrix_rows):
    block_size = min(512, query_matrix_rows.shape[0])
    pieces = query_matrix_rows.reshape(
        query_matrix_rows.shape[0] // block_size,
        block_size,
        query_matrix_rows.shape[1],
        query_matrix_rows.shape[2],
    )

    def one_block(one_piece):
        return attend_segment(one_piece, key_matrix_rows, value_matrix_rows)

    weighted, total, row_max = lax.map(one_block, pieces)
    return (
        weighted.reshape(query_matrix_rows.shape),
        total.reshape(query_matrix_rows.shape[:2]),
        row_max.reshape(query_matrix_rows.shape[:2]),
    )


def picked_rows(block_rows, offsets, stride):
    group_count = block_rows.shape[0] // stride
    grouped = block_rows.reshape(group_count, stride, block_rows.shape[1], block_rows.shape[2])
    chosen = (
        jnp.arange(stride, dtype=jnp.int32)[None, :, None, None] == offsets[None, None, :, None]
    )
    return jnp.sum(jnp.where(chosen, grouped, jnp.zeros((), grouped.dtype)), axis=1)


def scatter_rows(values, offsets, stride, filler):
    chosen = jnp.arange(stride, dtype=jnp.int32)[:, None] == offsets[None, :]
    spread_out = jnp.where(chosen[None], values[:, None], filler)
    return spread_out.reshape((values.shape[0] * stride,) + values.shape[1:])


def flatten_level(result):
    row_total = result[0].shape[0]
    weighted = result[0].reshape(row_total, -1)
    total = jnp.repeat(result[1], HD, axis=1)
    row_max = jnp.repeat(result[2], HD, axis=1)
    return (weighted, total, row_max)


def scatter_level(result, offsets, stride):
    weighted, total, row_max = flatten_level(result)
    column_offsets = jnp.repeat(offsets, HD)
    return (
        scatter_rows(weighted, column_offsets, stride, 0.0),
        scatter_rows(total, column_offsets, stride, 0.0),
        scatter_rows(row_max, column_offsets, stride, -jnp.inf),
    )


def combine(levels):
    highest = levels[0][2]
    for one_level in levels[1:]:
        highest = jnp.maximum(highest, one_level[2])
    numerator = jnp.zeros(levels[0][0].shape, jnp.float32)
    denominator = jnp.zeros(levels[0][1].shape, jnp.float32)
    for one_level in levels:
        factor = jnp.exp(one_level[2] - highest)
        numerator = numerator + factor * one_level[0]
        denominator = denominator + factor * one_level[1]
    return (numerator / denominator).astype(jnp.bfloat16)


def per_device(query, key, value, middle_offsets, upper_offsets, out_weight):
    row_count = query.shape[0]
    head_count = query.shape[1] // HD
    top_stride = lax.axis_size("seq") // 2
    query_matrix_rows = query.reshape(row_count, head_count, HD)
    key_matrix_rows = key.reshape(row_count, head_count, HD)
    value_matrix_rows = value.reshape(row_count, head_count, HD)
    top_key_local = picked_rows(key_matrix_rows, upper_offsets, top_stride).reshape(
        -1, head_count * HD
    )
    top_value_local = picked_rows(value_matrix_rows, upper_offsets, top_stride).reshape(
        -1, head_count * HD
    )
    top_key_all, top_value_all = (
        lax.all_gather(top_key_local, "seq", axis=0, tiled=True),
        lax.all_gather(top_value_local, "seq", axis=0, tiled=True),
    )
    upper_level = attend_segment(
        picked_rows(query_matrix_rows, upper_offsets, top_stride),
        top_key_all.reshape(-1, head_count, HD),
        top_value_all.reshape(-1, head_count, HD),
    )
    middle_pair = jnp.stack(
        [
            picked_rows(key_matrix_rows, middle_offsets, MIDDLE_DILATION),
            picked_rows(value_matrix_rows, middle_offsets, MIDDLE_DILATION),
        ]
    ).reshape(2, -1, head_count * HD)
    for bit_number in range(SPAN.bit_length() - 1):
        partner = partner_2(middle_pair, "seq", bit_number)
        middle_pair = jnp.concatenate([middle_pair, partner], axis=1)
    middle_level = attend_segment(
        picked_rows(query_matrix_rows, middle_offsets, MIDDLE_DILATION),
        middle_pair[0].reshape(-1, head_count, HD),
        middle_pair[1].reshape(-1, head_count, HD),
    )
    bottom = flatten_level(attend_blocks(query_matrix_rows, key_matrix_rows, value_matrix_rows))
    attention = combine(
        (
            bottom,
            scatter_level(middle_level, middle_offsets, MIDDLE_DILATION),
            scatter_level(upper_level, upper_offsets, top_stride),
        )
    )
    summed = lax.psum_scatter(
        jnp.dot(attention, out_weight, preferred_element_type=jnp.float32),
        "head",
        scatter_dimension=0,
        tiled=True,
    )
    return summed.astype(jnp.bfloat16)


MESH = pl.DeviceIdType.MESH
SHARED_ROWS = 96


def dot_f32(left, right):
    return jnp.dot(left, right, preferred_element_type=jnp.float32)


def three_parts(value):
    high = value.astype(jnp.bfloat16).astype(jnp.float32)
    rest = value - high
    middle = rest.astype(jnp.bfloat16).astype(jnp.float32)
    return [high, middle, rest - middle]


def softmax_of(scores):
    row_max = jnp.max(scores, axis=0, keepdims=True)
    return row_max, jnp.exp(scores - row_max).astype(jnp.bfloat16)


def weigh(values_with_ones, row_max, mass):
    summed = dot_f32(values_with_ones, mass)
    total = summed[HD : HD + 1]
    weighted = (summed[:HD] * (1.0 / total)).astype(jnp.bfloat16)
    return weighted, row_max + jnp.log(total)


def with_ones(values_t):
    ones = jnp.ones((16, values_t.shape[1]), values_t.dtype)
    return jnp.concatenate([values_t, ones], axis=0)


def pipelined(units, ahead, lag):
    scores, masses = {}, {}
    for i in range(len(units) + ahead + lag):
        if i < len(units):
            scores[i] = units[i][0]()
        j = i - ahead
        if 0 <= j < len(units):
            soften = units[j][2] if len(units[j]) > 2 else softmax_of
            masses[j] = soften(scores.pop(j))
        k = j - lag
        if 0 <= k < len(units):
            units[k][1](*masses.pop(k))


def select_half(block, which):
    blank = jnp.zeros_like(block)
    return jnp.concatenate([blank, block] if which else [block, blank], axis=0)


def fused_kernel(
    seq_total,
    query_hbm,
    key_hbm,
    value_hbm,
    middle_hbm,
    upper_hbm,
    weight_hbm,
    out_ref,
    query_ref,
    key_ref,
    value_ref,
    middle_ref,
    upper_ref,
    load,
    query_t,
    select,
    sent_kv,
    sent_q,
    got_kv,
    got_q,
    result,
    result_stat,
    returned,
    returned_stat,
    bottom,
    bottom_stat,
    bottom_got,
    bottom_stat_got,
    weights,
    attention,
    send_kv,
    recv_kv,
    send_q,
    recv_q,
    send_back,
    recv_back,
    send_stat,
    recv_stat,
    send_bottom,
    recv_bottom,
    send_weight,
    recv_weight,
):
    seq, head = lax.axis_index("seq"), lax.axis_index("head")
    chip, core = lax.div(head, 2), lax.rem(head, 2)
    beside_head = 2 * chip + (1 - core)
    across_head = 2 * (1 - chip) + core
    y = lax.rem(seq, 2)
    y_peer = seq + 1 - 2 * y
    rows = query_ref.shape[0]
    heads = query_ref.shape[1] // HD
    taken = rows // MIDDLE_DILATION
    part = taken // 4
    half_total = seq_total // 2
    offset_refs = (middle_ref, upper_ref)
    my_half, my_low = lax.div(seq, half_total), lax.rem(seq, half_total)
    my_inner = lax.rem(lax.div(seq, 2) + my_half, 2)

    def target_of(slot):
        half = lax.rem(my_half + slot // half_total, 2)
        return half * half_total + lax.rem(my_low + slot % half_total, half_total)

    z = lax.div(seq, 2)
    my_inner = lax.rem(z + my_half, 2)

    loads = []
    for i, (source, target) in enumerate(
        (
            (value_hbm, value_ref),
            (key_hbm, key_ref),
            (middle_hbm, middle_ref),
            (upper_hbm, upper_ref),
            (query_hbm, query_ref),
            (weight_hbm, weights.at[head]),
        )
    ):
        loads.append(pltpu.make_async_copy(source, target, load.at[i]))
    for copy in loads[:4]:
        copy.start()

    barrier = pltpu.get_barrier_semaphore()
    for step in range(1, seq_total):
        pl.semaphore_signal(
            barrier,
            inc=1,
            device_id=(lax.rem(seq + step, seq_total), head),
            device_id_type=MESH,
        )
    for step in range(1, 4):
        pl.semaphore_signal(
            barrier, inc=1, device_id=(seq, lax.rem(head + step, 4)), device_id_type=MESH
        )

    loads[4].start()
    distance = lax.broadcasted_iota(jnp.int32, (taken, rows), 1) - MIDDLE_DILATION * (
        lax.broadcasted_iota(jnp.int32, (taken, rows), 0)
    )

    def pick(source_t, one, chosen):
        return lax.dot_general(
            source_t[one * HD : (one + 1) * HD],
            chosen,
            (((1,), (1,)), ((), ())),
            preferred_element_type=jnp.float32,
        ).astype(jnp.bfloat16)

    for copy in loads[:4]:
        copy.wait()
    loads[5].start()
    value_t = value_ref[...].T
    for one in range(heads):
        for level in range(2):
            pair = level * heads + one
            chosen = jnp.where(
                distance == offset_refs[level][one], jnp.float32(1), jnp.float32(0)
            ).astype(jnp.bfloat16)
            select[pair] = chosen
            sent_kv[pair, 0:HD] = pick(value_t, one, chosen)
            picked = dot_f32(chosen, key_ref[:, one * HD : (one + 1) * HD])
            sent_kv[pair, HD : 2 * HD] = jnp.concatenate(
                [picked[: taken // 2], picked[taken // 2 :]], axis=1
            ).astype(jnp.bfloat16)

    def prepare_q():
        query_t[...] = (query_ref[...] * jnp.bfloat16(HD**-0.5)).T
        for one in range(heads):
            for level in range(2):
                pair = level * heads + one
                sent_q[pair] = pick(query_t, one, select[pair])

    loads[4].wait()
    pl.when(seq < EARLY_SHARDS)(prepare_q)
    pl.semaphore_wait(barrier, seq_total + 2)
    waits = []

    def send(source, target, send_sem, recv_sem, device):
        copy = pltpu.make_async_remote_copy(
            src_ref=source,
            dst_ref=target,
            send_sem=send_sem,
            recv_sem=recv_sem,
            device_id=device,
            device_id_type=MESH,
        )
        copy.start()
        return copy

    def send_kv_to(slot):
        to = target_of(slot)
        sem = recv_kv.at[my_inner] if slot >= half_total else recv_kv.at[2]
        waits.append(
            send(sent_kv.at[to], got_kv.at[seq], send_kv.at[slot], sem, (to, head))
        )

    def send_q_to(slot):
        to = target_of(slot)
        copy = pltpu.make_async_remote_copy(
            src_ref=sent_q.at[to],
            dst_ref=got_q.at[seq],
            send_sem=send_q.at[slot],
            recv_sem=recv_q.at[seq],
            device_id=(to, head),
            device_id_type=MESH,
        )
        copy.start()

    def send_far_q():
        for slot in range(half_total, seq_total):
            send_q_to(slot)

    pl.when(seq < EARLY_SHARDS)(send_far_q)
    for slot in KV_ORDER:
        send_kv_to(slot)
    loads[5].wait()
    own_rows = weights.shape[1]
    middle_rows = own_rows - 2 * SHARED_ROWS
    mine = pl.ds(y * (own_rows - SHARED_ROWS), SHARED_ROWS)
    others = pl.ds((1 - y) * (own_rows - SHARED_ROWS), SHARED_ROWS)
    common = pl.ds(SHARED_ROWS, middle_rows)

    def send_weight_rows(which, part_rows, index, device):
        block = weights.at[which, part_rows]
        copy = send(block, block, send_weight.at[index], recv_weight.at[index], device)
        waits.append(copy)
        return copy

    def weight_arrived(which, part_rows, index):
        block = weights.at[which, part_rows]
        pltpu.make_async_copy(block, block, recv_weight.at[index]).wait()

    send_weight_rows(head, mine, 0, (seq, across_head))
    send_weight_rows(head, common, 1, (seq, across_head))
    send_weight_rows(head, pl.ds(0, own_rows), 3, (seq, beside_head))
    pl.when(seq >= EARLY_SHARDS)(prepare_q)
    got_kv[seq] = sent_kv[seq]
    own_q = pltpu.make_async_copy(sent_q.at[seq], got_q.at[seq], recv_q.at[seq])
    own_q.start()
    for slot in range(1, half_total):
        send_q_to(slot)
    in_between = jnp.logical_and(seq >= EARLY_SHARDS, seq < LATE_SHARDS)
    pl.when(in_between)(send_far_q)

    residue = lax.rem(lax.broadcasted_iota(jnp.int32, (1, taken), 1), MIDDLE_DILATION)
    half = rows // 2
    blocks = half // taken
    units = []
    for one in range(heads):
        for piece in range(2):

            def bottom_scores(one=one, piece=piece):
                both = slice(one // 2 * 2 * HD, (one // 2 + 1) * 2 * HD)
                block = query_t[one * HD : (one + 1) * HD, piece * half : (piece + 1) * half]
                return dot_f32(key_ref[:, both], select_half(block, one % 2))

            def bottom_sums(row_max, mass, one=one, piece=piece):
                span = slice(one * HD, (one + 1) * HD)
                weighted, logs = weigh(with_ones(value_t[span]), row_max, mass)
                for i in range(blocks):
                    cut = slice(i * taken, (i + 1) * taken)
                    bottom[piece * blocks + i, span] = weighted[:, cut]
                    bottom_stat[piece * blocks + i, one : one + 1] = logs[:, cut]

            units.append((bottom_scores, bottom_sums))
    pipelined(units, 2, 1)
    for one in range(heads):
        for level in range(2):
            bias = jnp.where(residue == offset_refs[level][one], 0.0, -jnp.inf)
            row = (level + 1) * heads + one
            for i in range(4):
                bottom_stat[i, row : row + 1] = bias
    for i in range(4):
        bottom_stat[i, 3 * heads :] = jnp.zeros((heads, taken), jnp.float32)

    for step in range(1, 4):
        to = lax.rem(head + step, 4)
        waits.append(
            send(
                bottom.at[to],
                bottom_got.at[head],
                send_bottom.at[step],
                recv_bottom.at[0],
                (seq, to),
            )
        )
        waits.append(
            send(
                bottom_stat.at[to],
                bottom_stat_got.at[head],
                send_bottom.at[4 + step],
                recv_bottom.at[1],
                (seq, to),
            )
        )
    bottom_got[head] = bottom[head]
    bottom_stat_got[head] = bottom_stat[head]

    def arrived(ref, count, sem):
        block = ref.at[pl.ds(0, count)]
        pltpu.make_async_copy(block, block, sem).wait()

    arrived(got_kv, 2, recv_kv.at[0])
    pl.when(seq >= LATE_SHARDS)(send_far_q)

    weight_arrived(across_head, mine, 0)
    send_weight_rows(across_head, mine, 2, (y_peer, head))
    send_weight_rows(across_head, mine, 4, (seq, beside_head))

    arrived(got_kv, 2, recv_kv.at[1])
    arrived(got_kv, half_total - 1, recv_kv.at[2])
    keys = jnp.concatenate([got_kv[i, HD : 2 * HD] for i in range(seq_total)], axis=0)
    values_t = with_ones(
        jnp.concatenate([got_kv[i, 0:HD] for i in range(seq_total)], axis=1)
    )
    place = lax.div(seq, heads) * (4 * heads) + head * heads + lax.rem(seq, heads)
    units, unless_own = [], []
    for slots in BLOCKS:

        def upper_scores(slots=slots):
            for slot in slots:
                block = got_q.at[slot]
                pltpu.make_async_copy(block, block, recv_q.at[slot]).wait()
            block = jnp.concatenate([got_q[slot] for slot in slots], axis=1)
            return [dot_f32(keys, select_half(block, which)) for which in range(2)]

        def upper_masses(scores):
            row_max = jnp.maximum(
                *[jnp.max(part_scores, axis=0, keepdims=True) for part_scores in scores]
            )
            masses = [
                jnp.exp(part_scores - row_max).astype(jnp.bfloat16) for part_scores in scores
            ]
            pieces = []
            for i in range(seq_total):
                for which in range(2):
                    pieces.append(masses[which][i * HD : (i + 1) * HD])
            return row_max, jnp.concatenate(pieces, axis=0)

        def upper_sums(row_max, mass, slots=slots):
            weighted, logs = weigh(values_t, row_max, mass)
            for slot, begin in zip(slots, range(0, len(slots) * taken, taken)):
                for i in range(4):
                    lanes = slice(begin + i * part, begin + (i + 1) * part)
                    result[slot, i] = jnp.concatenate(
                        [weighted[16 * c : 16 * (c + 1), lanes] for c in range(4)], axis=1
                    )
                result_stat[slot] = logs[:, begin : begin + taken]
                for step in (1, 2, 3, 0):
                    i = lax.rem(head + step, 4)
                    pair_of_copies = [
                        pltpu.make_async_remote_copy(
                            src_ref=source,
                            dst_ref=target.at[place],
                            send_sem=sems.at[slot, step],
                            recv_sem=recv_sem,
                            device_id=(slot, i),
                            device_id_type=MESH,
                        )
                        for source, target, sems, recv_sem in (
                            (result.at[slot, i], returned, send_back, recv_back),
                            (result_stat.at[slot], returned_stat, send_stat, recv_stat),
                        )
                    ]
                    for copy in pair_of_copies:
                        if step:
                            copy.start()
                            waits.append(copy)
                        else:
                            pl.when(slot != seq)(copy.start)
                            unless_own.append((slot, copy))

                @pl.when(slot == seq)
                def _():
                    returned[place] = result[slot, head]
                    returned_stat[place] = result_stat[slot]

        units.append((upper_scores, upper_sums, upper_masses))
    pipelined(units[:ALONE], 0, 0)
    pipelined(units[ALONE:], *UPPER_DEPTH)

    weight_arrived(across_head, common, 1)
    send_weight_rows(across_head, common, 5, (seq, beside_head))
    weight_arrived(across_head, others, 2)
    send_weight_rows(across_head, others, 6, (seq, beside_head))

    repeat = (
        (
            lax.broadcasted_iota(jnp.int32, (taken, rows), 0)
            == part * (lax.broadcasted_iota(jnp.int32, (taken, rows), 1) // taken)
            + (lax.broadcasted_iota(jnp.int32, (taken, rows), 1) % taken) // MIDDLE_DILATION
        )
        .astype(jnp.float32)
        .astype(jnp.bfloat16)
    )
    repeat_stat = (
        (
            lax.broadcasted_iota(jnp.int32, (taken, taken), 0)
            == part * head + lax.broadcasted_iota(jnp.int32, (taken, taken), 1) // MIDDLE_DILATION
        )
        .astype(jnp.float32)
        .astype(jnp.bfloat16)
    )
    arrived(bottom_got, 3, recv_bottom.at[0])
    arrived(bottom_stat_got, 3, recv_bottom.at[1])
    pairs = returned.shape[0]
    arrived(returned_stat, pairs - 1, recv_stat)
    logs = sum(
        dot_f32(value.astype(jnp.bfloat16), repeat_stat)
        for value in three_parts(returned_stat[...].reshape(pairs, taken))
    )

    def stat_rows(begin):
        return jnp.concatenate(
            [bottom_stat_got[i, begin : begin + heads] for i in range(4)], axis=0
        )

    all_logs = [stat_rows(0)]
    for level in range(2):
        level_logs = logs[level * 4 * heads : (level + 1) * 4 * heads]
        all_logs.append(level_logs + stat_rows((level + 1) * heads))
    highest = jnp.maximum(jnp.maximum(all_logs[0], all_logs[1]), all_logs[2])
    factors = [jnp.exp(one_log - highest) for one_log in all_logs]
    inverse = 1.0 / (factors[0] + factors[1] + factors[2])
    factors = [factor * inverse for factor in factors]

    weight_arrived(beside_head, pl.ds(0, own_rows), 3)
    diagonal = 2 * (1 - chip) + (1 - core)
    weight_arrived(diagonal, mine, 4)
    weight_arrived(diagonal, common, 5)
    weight_arrived(diagonal, others, 6)
    arrived(returned, pairs - 1, recv_back)
    spread = dot_f32(returned[...].reshape(pairs * 16, taken), repeat)
    for one in range(4 * heads):
        for c in range(4):
            lanes = slice(c * taken, (c + 1) * taken)
            begin = (one % heads) * HD + 16 * c
            total = factors[0][one : one + 1] * bottom_got[
                one // heads, begin : begin + 16
            ].astype(jnp.float32)
            for level in range(2):
                at = (level * 4 * heads + one) * 16
                total += factors[level + 1][one : one + 1] * spread[at : at + 16, lanes]
            attention[one * HD + 16 * c : one * HD + 16 * (c + 1)] = total.astype(
                jnp.bfloat16
            )

    projected = dot_f32(
        attention[...].T, weights[...].reshape(attention.shape[0], weights.shape[2])
    )
    out_ref[...] = projected.astype(out_ref.dtype)
    for copy in waits:
        copy.wait_send()
    for slot in range(1, seq_total):
        pltpu.make_async_copy(sent_q.at[0], sent_q.at[0], send_q.at[slot]).wait()
    for slot, copy in unless_own:
        pl.when(slot != seq)(copy.wait_send)


ALONE = 1
UPPER_DEPTH = (1, 0)
EARLY_SHARDS, LATE_SHARDS = 2, 8
KV_ORDER = (4, 5, 6, 7, 1, 2, 3)
BLOCKS = ((0,), (1,), (2, 3), (4, 5), (6, 7))


def per_device_fused(query, key, value, middle_offsets, upper_offsets, out_weight):
    rows, width = query.shape
    seq_total = lax.axis_size("seq")
    heads = width // HD
    pairs = 2 * heads
    taken = rows // MIDDLE_DILATION
    anywhere = pl.BlockSpec(memory_space=pl.ANY)
    dma = pltpu.SemaphoreType.DMA
    bf16, f32 = jnp.bfloat16, jnp.float32
    return pl.pallas_call(
        functools.partial(fused_kernel, seq_total),
        out_shape=pltpu.VMEM((rows // 4, out_weight.shape[1]), bf16),
        in_specs=[anywhere] * 6,
        out_specs=pl.BlockSpec(memory_space=pltpu.VMEM),
        scratch_shapes=[
            pltpu.VMEM(query.shape, query.dtype),
            pltpu.VMEM(key.shape, key.dtype),
            pltpu.VMEM(value.shape, value.dtype),
            pltpu.SMEM(middle_offsets.shape, jnp.int32),
            pltpu.SMEM(upper_offsets.shape, jnp.int32),
            dma((6,)),
            pltpu.VMEM((width, rows), bf16),
            pltpu.VMEM((pairs, taken, rows), bf16),
            pltpu.VMEM((pairs, 2 * HD, taken), bf16),
            pltpu.VMEM((pairs, HD, taken), bf16),
            pltpu.VMEM((seq_total, 2 * HD, taken), bf16),
            pltpu.VMEM((seq_total, HD, taken), bf16),
            pltpu.VMEM((seq_total, 4, 16, taken), bf16),
            pltpu.VMEM((seq_total, 1, taken), f32),
            pltpu.VMEM((4 * pairs, 16, taken), bf16),
            pltpu.VMEM((4 * pairs, 1, taken), f32),
            pltpu.VMEM((4, width, taken), bf16),
            pltpu.VMEM((4, 4 * heads, taken), f32),
            pltpu.VMEM((4, width, taken), bf16),
            pltpu.VMEM((4, 4 * heads, taken), f32),
            pltpu.VMEM((4,) + out_weight.shape, bf16),
            pltpu.VMEM((4 * width, taken), bf16),
            dma((seq_total,)),
            dma((3,)),
            dma((seq_total,)),
            dma((seq_total,)),
            dma((seq_total, 4)),
            dma,
            dma((seq_total, 4)),
            dma,
            dma((8,)),
            dma((2,)),
            dma((7,)),
            dma((7,)),
        ],
        compiler_params=pltpu.CompilerParams(
            collective_id=0, has_side_effects=True, vmem_limit_bytes=56 * 2**20
        ),
    )(query, key, value, middle_offsets, upper_offsets, out_weight)


def solution(mesh):
    in_specs = (
        P("seq", "head"),
        P("seq", "head"),
        P("seq", "head"),
        P("head"),
        P("head"),
        P("head", None),
    )
    out_specs = P(("seq", "head"), None)
    seq_total, head_shards = mesh.shape["seq"], mesh.shape["head"]
    one_segment = seq_total == SPAN and seq_total // 2 == MIDDLE_DILATION and head_shards == 4
    return jax.shard_map(
        per_device_fused if one_segment else per_device, mesh=mesh, in_specs=in_specs, out_specs=out_specs, check_vma=False
    )
```

```python
import functools

import jax
import jax.numpy as jnp
from jax import lax
from jax.experimental import pallas as pl
from jax.experimental.pallas import tpu as pltpu
from jax.sharding import PartitionSpec as P

HD = 64
SPAN = 8
MIDDLE_DILATION = 4


def partner_2(value, axis, stride):
    mask = 2**stride
    pairs = [(source, source ^ mask) for source in range(lax.axis_size(axis))]
    return lax.ppermute(value, axis, pairs)


def attend_segment(query_matrix_rows, key_matrix_rows, value_matrix_rows):
    scores = jnp.einsum(
        "qhd,khd->hqk", query_matrix_rows, key_matrix_rows, preferred_element_type=jnp.float32
    ) * HD ** (-0.5)
    row_max = jnp.max(scores, axis=2)
    mass = jnp.exp(scores - row_max[:, :, None])
    total = jnp.sum(mass, axis=2)
    soft_weights = mass.astype(jnp.bfloat16)
    weighted = jnp.einsum(
        "hqk,khd->qhd", soft_weights, value_matrix_rows, preferred_element_type=jnp.float32
    )
    return (weighted, total.T, row_max.T)


def attend_blocks(query_matrix_rows, key_matrix_rows, value_matrix_rows):
    block_size = min(512, query_matrix_rows.shape[0])
    pieces = query_matrix_rows.reshape(
        query_matrix_rows.shape[0] // block_size,
        block_size,
        query_matrix_rows.shape[1],
        query_matrix_rows.shape[2],
    )

    def one_block(one_piece):
        return attend_segment(one_piece, key_matrix_rows, value_matrix_rows)

    weighted, total, row_max = lax.map(one_block, pieces)
    return (
        weighted.reshape(query_matrix_rows.shape),
        total.reshape(query_matrix_rows.shape[:2]),
        row_max.reshape(query_matrix_rows.shape[:2]),
    )


def picked_rows(block_rows, offsets, stride):
    group_count = block_rows.shape[0] // stride
    grouped = block_rows.reshape(group_count, stride, block_rows.shape[1], block_rows.shape[2])
    chosen = (
        jnp.arange(stride, dtype=jnp.int32)[None, :, None, None] == offsets[None, None, :, None]
    )
    return jnp.sum(jnp.where(chosen, grouped, jnp.zeros((), grouped.dtype)), axis=1)


def scatter_rows(values, offsets, stride, filler):
    chosen = jnp.arange(stride, dtype=jnp.int32)[:, None] == offsets[None, :]
    spread_out = jnp.where(chosen[None], values[:, None], filler)
    return spread_out.reshape((values.shape[0] * stride,) + values.shape[1:])


def flatten_level(result):
    row_total = result[0].shape[0]
    weighted = result[0].reshape(row_total, -1)
    total = jnp.repeat(result[1], HD, axis=1)
    row_max = jnp.repeat(result[2], HD, axis=1)
    return (weighted, total, row_max)


def scatter_level(result, offsets, stride):
    weighted, total, row_max = flatten_level(result)
    column_offsets = jnp.repeat(offsets, HD)
    return (
        scatter_rows(weighted, column_offsets, stride, 0.0),
        scatter_rows(total, column_offsets, stride, 0.0),
        scatter_rows(row_max, column_offsets, stride, -jnp.inf),
    )


def combine(levels):
    highest = levels[0][2]
    for one_level in levels[1:]:
        highest = jnp.maximum(highest, one_level[2])
    numerator = jnp.zeros(levels[0][0].shape, jnp.float32)
    denominator = jnp.zeros(levels[0][1].shape, jnp.float32)
    for one_level in levels:
        factor = jnp.exp(one_level[2] - highest)
        numerator = numerator + factor * one_level[0]
        denominator = denominator + factor * one_level[1]
    return (numerator / denominator).astype(jnp.bfloat16)


def per_device(query, key, value, middle_offsets, upper_offsets, out_weight):
    row_count = query.shape[0]
    head_count = query.shape[1] // HD
    top_stride = lax.axis_size("seq") // 2
    query_matrix_rows = query.reshape(row_count, head_count, HD)
    key_matrix_rows = key.reshape(row_count, head_count, HD)
    value_matrix_rows = value.reshape(row_count, head_count, HD)
    top_key_local = picked_rows(key_matrix_rows, upper_offsets, top_stride).reshape(
        -1, head_count * HD
    )
    top_value_local = picked_rows(value_matrix_rows, upper_offsets, top_stride).reshape(
        -1, head_count * HD
    )
    top_key_all, top_value_all = (
        lax.all_gather(top_key_local, "seq", axis=0, tiled=True),
        lax.all_gather(top_value_local, "seq", axis=0, tiled=True),
    )
    upper_level = attend_segment(
        picked_rows(query_matrix_rows, upper_offsets, top_stride),
        top_key_all.reshape(-1, head_count, HD),
        top_value_all.reshape(-1, head_count, HD),
    )
    middle_pair = jnp.stack(
        [
            picked_rows(key_matrix_rows, middle_offsets, MIDDLE_DILATION),
            picked_rows(value_matrix_rows, middle_offsets, MIDDLE_DILATION),
        ]
    ).reshape(2, -1, head_count * HD)
    for bit_number in range(SPAN.bit_length() - 1):
        partner = partner_2(middle_pair, "seq", bit_number)
        middle_pair = jnp.concatenate([middle_pair, partner], axis=1)
    middle_level = attend_segment(
        picked_rows(query_matrix_rows, middle_offsets, MIDDLE_DILATION),
        middle_pair[0].reshape(-1, head_count, HD),
        middle_pair[1].reshape(-1, head_count, HD),
    )
    bottom = flatten_level(attend_blocks(query_matrix_rows, key_matrix_rows, value_matrix_rows))
    attention = combine(
        (
            bottom,
            scatter_level(middle_level, middle_offsets, MIDDLE_DILATION),
            scatter_level(upper_level, upper_offsets, top_stride),
        )
    )
    summed = lax.psum_scatter(
        jnp.dot(attention, out_weight, preferred_element_type=jnp.float32),
        "head",
        scatter_dimension=0,
        tiled=True,
    )
    return summed.astype(jnp.bfloat16)


MESH = pl.DeviceIdType.MESH
SHARED_ROWS = 96


def dot_f32(left, right):
    return jnp.dot(left, right, preferred_element_type=jnp.float32)


def three_parts(value):
    high = value.astype(jnp.bfloat16).astype(jnp.float32)
    rest = value - high
    middle = rest.astype(jnp.bfloat16).astype(jnp.float32)
    return [high, middle, rest - middle]


def softmax_of(scores):
    row_max = jnp.max(scores, axis=0, keepdims=True)
    return row_max, jnp.exp(scores - row_max).astype(jnp.bfloat16)


def weigh(values_with_ones, row_max, mass):
    summed = dot_f32(values_with_ones, mass)
    total = summed[HD : HD + 1]
    weighted = (summed[:HD] * (1.0 / total)).astype(jnp.bfloat16)
    return weighted, row_max + jnp.log(total)


def with_ones(values_t):
    ones = jnp.ones((16, values_t.shape[1]), values_t.dtype)
    return jnp.concatenate([values_t, ones], axis=0)


def pipelined(units, ahead, lag):
    scores, masses = {}, {}
    for i in range(len(units) + ahead + lag):
        if i < len(units):
            scores[i] = units[i][0]()
        j = i - ahead
        if 0 <= j < len(units):
            soften = units[j][2] if len(units[j]) > 2 else softmax_of
            masses[j] = soften(scores.pop(j))
        k = j - lag
        if 0 <= k < len(units):
            units[k][1](*masses.pop(k))


def select_half(block, which):
    blank = jnp.zeros_like(block)
    return jnp.concatenate([blank, block] if which else [block, blank], axis=0)


def fused_kernel(
    seq_total,
    query_hbm,
    key_hbm,
    value_hbm,
    middle_hbm,
    upper_hbm,
    weight_hbm,
    out_ref,
    query_ref,
    key_ref,
    value_ref,
    middle_ref,
    upper_ref,
    load,
    query_t,
    select,
    sent_kv,
    sent_q,
    got_kv,
    got_q,
    result,
    result_stat,
    returned,
    returned_stat,
    bottom,
    bottom_stat,
    bottom_got,
    bottom_stat_got,
    weights,
    attention,
    send_kv,
    recv_kv,
    send_q,
    recv_q,
    send_back,
    recv_back,
    send_stat,
    recv_stat,
    send_bottom,
    recv_bottom,
    send_weight,
    recv_weight,
):
    seq, head = lax.axis_index("seq"), lax.axis_index("head")
    chip, core = lax.div(head, 2), lax.rem(head, 2)
    beside_head = 2 * chip + (1 - core)
    across_head = 2 * (1 - chip) + core
    y = lax.rem(seq, 2)
    y_peer = seq + 1 - 2 * y
    rows = query_ref.shape[0]
    heads = query_ref.shape[1] // HD
    taken = rows // MIDDLE_DILATION
    part = taken // 4
    half_total = seq_total // 2
    offset_refs = (middle_ref, upper_ref)
    my_half, my_low = lax.div(seq, half_total), lax.rem(seq, half_total)
    my_inner = lax.rem(lax.div(seq, 2) + my_half, 2)

    def target_of(slot):
        half = lax.rem(my_half + slot // half_total, 2)
        return half * half_total + lax.rem(my_low + slot % half_total, half_total)

    z = lax.div(seq, 2)
    my_inner = lax.rem(z + my_half, 2)

    loads = []
    for i, (source, target) in enumerate(
        (
            (value_hbm, value_ref),
            (key_hbm, key_ref),
            (middle_hbm, middle_ref),
            (upper_hbm, upper_ref),
            (query_hbm, query_ref),
            (weight_hbm, weights.at[head]),
        )
    ):
        loads.append(pltpu.make_async_copy(source, target, load.at[i]))
    for copy in loads[:4]:
        copy.start()

    barrier = pltpu.get_barrier_semaphore()
    for step in range(1, seq_total):
        pl.semaphore_signal(
            barrier,
            inc=1,
            device_id=(lax.rem(seq + step, seq_total), head),
            device_id_type=MESH,
        )
    for step in range(1, 4):
        pl.semaphore_signal(
            barrier, inc=1, device_id=(seq, lax.rem(head + step, 4)), device_id_type=MESH
        )

    loads[4].start()
    distance = lax.broadcasted_iota(jnp.int32, (taken, rows), 1) - MIDDLE_DILATION * (
        lax.broadcasted_iota(jnp.int32, (taken, rows), 0)
    )

    def pick(source_t, one, chosen):
        return lax.dot_general(
            source_t[one * HD : (one + 1) * HD],
            chosen,
            (((1,), (1,)), ((), ())),
            preferred_element_type=jnp.float32,
        ).astype(jnp.bfloat16)

    for copy in loads[:4]:
        copy.wait()
    loads[5].start()
    value_t = value_ref[...].T
    for one in range(heads):
        for level in range(2):
            pair = level * heads + one
            chosen = jnp.where(
                distance == offset_refs[level][one], jnp.float32(1), jnp.float32(0)
            ).astype(jnp.bfloat16)
            select[pair] = chosen
            sent_kv[pair, 0:HD] = pick(value_t, one, chosen)
            picked = dot_f32(chosen, key_ref[:, one * HD : (one + 1) * HD])
            sent_kv[pair, HD : 2 * HD] = jnp.concatenate(
                [picked[: taken // 2], picked[taken // 2 :]], axis=1
            ).astype(jnp.bfloat16)

    def prepare_q():
        query_t[...] = (query_ref[...] * jnp.bfloat16(HD**-0.5)).T
        for one in range(heads):
            for level in range(2):
                pair = level * heads + one
                sent_q[pair] = pick(query_t, one, select[pair])

    loads[4].wait()
    pl.when(seq < EARLY_SHARDS)(prepare_q)
    pl.semaphore_wait(barrier, seq_total + 2)
    waits = []

    def send(source, target, send_sem, recv_sem, device):
        copy = pltpu.make_async_remote_copy(
            src_ref=source,
            dst_ref=target,
            send_sem=send_sem,
            recv_sem=recv_sem,
            device_id=device,
            device_id_type=MESH,
        )
        copy.start()
        return copy

    def send_kv_to(slot):
        to = target_of(slot)
        sem = recv_kv.at[my_inner] if slot >= half_total else recv_kv.at[2]
        waits.append(
            send(sent_kv.at[to], got_kv.at[seq], send_kv.at[slot], sem, (to, head))
        )

    def send_q_to(slot):
        to = target_of(slot)
        copy = pltpu.make_async_remote_copy(
            src_ref=sent_q.at[to],
            dst_ref=got_q.at[seq],
            send_sem=send_q.at[slot],
            recv_sem=recv_q.at[seq],
            device_id=(to, head),
            device_id_type=MESH,
        )
        copy.start()

    def send_far_q():
        for slot in range(half_total, seq_total):
            send_q_to(slot)

    pl.when(seq < EARLY_SHARDS)(send_far_q)
    for slot in KV_ORDER:
        send_kv_to(slot)
    loads[5].wait()
    own_rows = weights.shape[1]
    middle_rows = own_rows - 2 * SHARED_ROWS
    mine = pl.ds(y * (own_rows - SHARED_ROWS), SHARED_ROWS)
    others = pl.ds((1 - y) * (own_rows - SHARED_ROWS), SHARED_ROWS)
    common = pl.ds(SHARED_ROWS, middle_rows)

    def send_weight_rows(which, part_rows, index, device):
        block = weights.at[which, part_rows]
        copy = send(block, block, send_weight.at[index], recv_weight.at[index], device)
        waits.append(copy)
        return copy

    def weight_arrived(which, part_rows, index):
        block = weights.at[which, part_rows]
        pltpu.make_async_copy(block, block, recv_weight.at[index]).wait()

    send_weight_rows(head, mine, 0, (seq, across_head))
    send_weight_rows(head, common, 1, (seq, across_head))
    send_weight_rows(head, pl.ds(0, own_rows), 3, (seq, beside_head))
    pl.when(seq >= EARLY_SHARDS)(prepare_q)
    got_kv[seq] = sent_kv[seq]
    own_q = pltpu.make_async_copy(sent_q.at[seq], got_q.at[seq], recv_q.at[seq])
    own_q.start()
    for slot in range(1, half_total):
        send_q_to(slot)
    in_between = jnp.logical_and(seq >= EARLY_SHARDS, seq < LATE_SHARDS)
    pl.when(in_between)(send_far_q)

    residue = lax.rem(lax.broadcasted_iota(jnp.int32, (1, taken), 1), MIDDLE_DILATION)
    half = rows // 2
    blocks = half // taken
    units = []
    for one in range(heads):
        for piece in range(2):

            def bottom_scores(one=one, piece=piece):
                both = slice(one // 2 * 2 * HD, (one // 2 + 1) * 2 * HD)
                block = query_t[one * HD : (one + 1) * HD, piece * half : (piece + 1) * half]
                return dot_f32(key_ref[:, both], select_half(block, one % 2))

            def bottom_sums(row_max, mass, one=one, piece=piece):
                span = slice(one * HD, (one + 1) * HD)
                weighted, logs = weigh(with_ones(value_t[span]), row_max, mass)
                for i in range(blocks):
                    cut = slice(i * taken, (i + 1) * taken)
                    bottom[piece * blocks + i, span] = weighted[:, cut]
                    bottom_stat[piece * blocks + i, one : one + 1] = logs[:, cut]

            units.append((bottom_scores, bottom_sums))
    pipelined(units, 2, 1)
    for one in range(heads):
        for level in range(2):
            bias = jnp.where(residue == offset_refs[level][one], 0.0, -jnp.inf)
            row = (level + 1) * heads + one
            for i in range(4):
                bottom_stat[i, row : row + 1] = bias
    for i in range(4):
        bottom_stat[i, 3 * heads :] = jnp.zeros((heads, taken), jnp.float32)

    for step in range(1, 4):
        to = lax.rem(head + step, 4)
        waits.append(
            send(
                bottom.at[to],
                bottom_got.at[head],
                send_bottom.at[step],
                recv_bottom.at[0],
                (seq, to),
            )
        )
        waits.append(
            send(
                bottom_stat.at[to],
                bottom_stat_got.at[head],
                send_bottom.at[4 + step],
                recv_bottom.at[1],
                (seq, to),
            )
        )
    bottom_got[head] = bottom[head]
    bottom_stat_got[head] = bottom_stat[head]

    def arrived(ref, count, sem):
        block = ref.at[pl.ds(0, count)]
        pltpu.make_async_copy(block, block, sem).wait()

    arrived(got_kv, 2, recv_kv.at[0])
    pl.when(seq >= LATE_SHARDS)(send_far_q)

    weight_arrived(across_head, mine, 0)
    send_weight_rows(across_head, mine, 2, (y_peer, head))
    send_weight_rows(across_head, mine, 4, (seq, beside_head))

    arrived(got_kv, 2, recv_kv.at[1])
    arrived(got_kv, half_total - 1, recv_kv.at[2])
    keys = jnp.concatenate([got_kv[i, HD : 2 * HD] for i in range(seq_total)], axis=0)
    values_t = with_ones(
        jnp.concatenate([got_kv[i, 0:HD] for i in range(seq_total)], axis=1)
    )
    place = lax.div(seq, heads) * (4 * heads) + head * heads + lax.rem(seq, heads)
    units, unless_own = [], []
    for slots in BLOCKS:

        def upper_scores(slots=slots):
            for slot in slots:
                block = got_q.at[slot]
                pltpu.make_async_copy(block, block, recv_q.at[slot]).wait()
            block = jnp.concatenate([got_q[slot] for slot in slots], axis=1)
            return [dot_f32(keys, select_half(block, which)) for which in range(2)]

        def upper_masses(scores):
            row_max = jnp.maximum(
                *[jnp.max(part_scores, axis=0, keepdims=True) for part_scores in scores]
            )
            masses = [
                jnp.exp(part_scores - row_max).astype(jnp.bfloat16) for part_scores in scores
            ]
            pieces = []
            for i in range(seq_total):
                for which in range(2):
                    pieces.append(masses[which][i * HD : (i + 1) * HD])
            return row_max, jnp.concatenate(pieces, axis=0)

        def upper_sums(row_max, mass, slots=slots):
            weighted, logs = weigh(values_t, row_max, mass)
            for slot, begin in zip(slots, range(0, len(slots) * taken, taken)):
                for i in range(4):
                    lanes = slice(begin + i * part, begin + (i + 1) * part)
                    result[slot, i] = jnp.concatenate(
                        [weighted[16 * c : 16 * (c + 1), lanes] for c in range(4)], axis=1
                    )
                result_stat[slot] = logs[:, begin : begin + taken]
                for step in (1, 2, 3, 0):
                    i = lax.rem(head + step, 4)
                    pair_of_copies = [
                        pltpu.make_async_remote_copy(
                            src_ref=source,
                            dst_ref=target.at[place],
                            send_sem=sems.at[slot, step],
                            recv_sem=recv_sem,
                            device_id=(slot, i),
                            device_id_type=MESH,
                        )
                        for source, target, sems, recv_sem in (
                            (result.at[slot, i], returned, send_back, recv_back),
                            (result_stat.at[slot], returned_stat, send_stat, recv_stat),
                        )
                    ]
                    for copy in pair_of_copies:
                        if step:
                            copy.start()
                            waits.append(copy)
                        else:
                            pl.when(slot != seq)(copy.start)
                            unless_own.append((slot, copy))

                @pl.when(slot == seq)
                def _():
                    returned[place] = result[slot, head]
                    returned_stat[place] = result_stat[slot]

        units.append((upper_scores, upper_sums, upper_masses))
    pipelined(units[:ALONE], 0, 0)
    pipelined(units[ALONE:], *UPPER_DEPTH)

    weight_arrived(across_head, common, 1)
    send_weight_rows(across_head, common, 5, (seq, beside_head))
    weight_arrived(across_head, others, 2)
    send_weight_rows(across_head, others, 6, (seq, beside_head))

    repeat = (
        (
            lax.broadcasted_iota(jnp.int32, (taken, rows), 0)
            == part * (lax.broadcasted_iota(jnp.int32, (taken, rows), 1) // taken)
            + (lax.broadcasted_iota(jnp.int32, (taken, rows), 1) % taken) // MIDDLE_DILATION
        )
        .astype(jnp.float32)
        .astype(jnp.bfloat16)
    )
    repeat_stat = (
        (
            lax.broadcasted_iota(jnp.int32, (taken, taken), 0)
            == part * head + lax.broadcasted_iota(jnp.int32, (taken, taken), 1) // MIDDLE_DILATION
        )
        .astype(jnp.float32)
        .astype(jnp.bfloat16)
    )
    arrived(bottom_got, 3, recv_bottom.at[0])
    arrived(bottom_stat_got, 3, recv_bottom.at[1])
    pairs = returned.shape[0]
    arrived(returned_stat, pairs - 1, recv_stat)
    logs = sum(
        dot_f32(value.astype(jnp.bfloat16), repeat_stat)
        for value in three_parts(returned_stat[...].reshape(pairs, taken))
    )

    def stat_rows(begin):
        return jnp.concatenate(
            [bottom_stat_got[i, begin : begin + heads] for i in range(4)], axis=0
        )

    all_logs = [stat_rows(0)]
    for level in range(2):
        level_logs = logs[level * 4 * heads : (level + 1) * 4 * heads]
        all_logs.append(level_logs + stat_rows((level + 1) * heads))
    highest = jnp.maximum(jnp.maximum(all_logs[0], all_logs[1]), all_logs[2])
    factors = [jnp.exp(one_log - highest) for one_log in all_logs]
    inverse = 1.0 / (factors[0] + factors[1] + factors[2])
    factors = [factor * inverse for factor in factors]

    weight_arrived(beside_head, pl.ds(0, own_rows), 3)
    diagonal = 2 * (1 - chip) + (1 - core)
    weight_arrived(diagonal, mine, 4)
    weight_arrived(diagonal, common, 5)
    weight_arrived(diagonal, others, 6)
    arrived(returned, pairs - 1, recv_back)
    spread = dot_f32(returned[...].reshape(pairs * 16, taken), repeat)
    for one in range(4 * heads):
        for c in range(4):
            lanes = slice(c * taken, (c + 1) * taken)
            begin = (one % heads) * HD + 16 * c
            total = factors[0][one : one + 1] * bottom_got[
                one // heads, begin : begin + 16
            ].astype(jnp.float32)
            for level in range(2):
                at = (level * 4 * heads + one) * 16
                total += factors[level + 1][one : one + 1] * spread[at : at + 16, lanes]
            attention[one * HD + 16 * c : one * HD + 16 * (c + 1)] = total.astype(
                jnp.bfloat16
            )

    projected = dot_f32(
        attention[...].T, weights[...].reshape(attention.shape[0], weights.shape[2])
    )
    out_ref[...] = projected.astype(out_ref.dtype)
    for copy in waits:
        copy.wait_send()
    for slot in range(1, seq_total):
        pltpu.make_async_copy(sent_q.at[0], sent_q.at[0], send_q.at[slot]).wait()
    for slot, copy in unless_own:
        pl.when(slot != seq)(copy.wait_send)


ALONE = 1
UPPER_DEPTH = (1, 0)
EARLY_SHARDS, LATE_SHARDS = 1, 8
KV_ORDER = (5, 4, 7, 6, 1, 2, 3)
BLOCKS = ((0,), (1,), (2, 3), (4, 5), (6, 7))


def per_device_fused(query, key, value, middle_offsets, upper_offsets, out_weight):
    rows, width = query.shape
    seq_total = lax.axis_size("seq")
    heads = width // HD
    pairs = 2 * heads
    taken = rows // MIDDLE_DILATION
    anywhere = pl.BlockSpec(memory_space=pl.ANY)
    dma = pltpu.SemaphoreType.DMA
    bf16, f32 = jnp.bfloat16, jnp.float32
    return pl.pallas_call(
        functools.partial(fused_kernel, seq_total),
        out_shape=pltpu.VMEM((rows // 4, out_weight.shape[1]), bf16),
        in_specs=[anywhere] * 6,
        out_specs=pl.BlockSpec(memory_space=pltpu.VMEM),
        scratch_shapes=[
            pltpu.VMEM(query.shape, query.dtype),
            pltpu.VMEM(key.shape, key.dtype),
            pltpu.VMEM(value.shape, value.dtype),
            pltpu.SMEM(middle_offsets.shape, jnp.int32),
            pltpu.SMEM(upper_offsets.shape, jnp.int32),
            dma((6,)),
            pltpu.VMEM((width, rows), bf16),
            pltpu.VMEM((pairs, taken, rows), bf16),
            pltpu.VMEM((pairs, 2 * HD, taken), bf16),
            pltpu.VMEM((pairs, HD, taken), bf16),
            pltpu.VMEM((seq_total, 2 * HD, taken), bf16),
            pltpu.VMEM((seq_total, HD, taken), bf16),
            pltpu.VMEM((seq_total, 4, 16, taken), bf16),
            pltpu.VMEM((seq_total, 1, taken), f32),
            pltpu.VMEM((4 * pairs, 16, taken), bf16),
            pltpu.VMEM((4 * pairs, 1, taken), f32),
            pltpu.VMEM((4, width, taken), bf16),
            pltpu.VMEM((4, 4 * heads, taken), f32),
            pltpu.VMEM((4, width, taken), bf16),
            pltpu.VMEM((4, 4 * heads, taken), f32),
            pltpu.VMEM((4,) + out_weight.shape, bf16),
            pltpu.VMEM((4 * width, taken), bf16),
            dma((seq_total,)),
            dma((3,)),
            dma((seq_total,)),
            dma((seq_total,)),
            dma((seq_total, 4)),
            dma,
            dma((seq_total, 4)),
            dma,
            dma((8,)),
            dma((2,)),
            dma((7,)),
            dma((7,)),
        ],
        compiler_params=pltpu.CompilerParams(
            collective_id=0, has_side_effects=True, vmem_limit_bytes=56 * 2**20
        ),
    )(query, key, value, middle_offsets, upper_offsets, out_weight)


def solution(mesh):
    in_specs = (
        P("seq", "head"),
        P("seq", "head"),
        P("seq", "head"),
        P("head"),
        P("head"),
        P("head", None),
    )
    out_specs = P(("seq", "head"), None)
    seq_total, head_shards = mesh.shape["seq"], mesh.shape["head"]
    one_segment = seq_total == SPAN and seq_total // 2 == MIDDLE_DILATION and head_shards == 4
    return jax.shard_map(
        per_device_fused if one_segment else per_device, mesh=mesh, in_specs=in_specs, out_specs=out_specs, check_vma=False
    )
```
